128 devices in a mesh: dp: 2 (over core), space: 64 (over y, z, x).
Axes of the slice: x: 4, y: 4, z: 4, core: 2. Of those that a mesh axis runs over, the one named last changes fastest.
Arguments:
- features: bfloat16 [2, 4096, 16, 1024], P('dp', 'space'), may hold values from -6 to 6
- psi: bfloat16 [2, 4096, 64, 256], P('dp', 'space'), may hold values from -0.75 to 0.75
- neighbors: int32 [2, 4096, 16], P('dp', 'space'), may hold values from 0 to 4095, as said below
- counts: int32 [2, 4096], P('dp', 'space'), may hold values from 4 to 16, as said below
- occupation: float32 [2, 256], P('dp'), may hold values from 0.1 to 1
- weights: bfloat16 [1024, 4096], P(None, 'space'), may hold values from -0.1875 to 0.1875
Outputs:
- energies: float32 [2, 256], P('dp')
- gradient: float32 [4096, 1024], P('space')
The draws below stay inside these ranges and needn't reach their ends.
Inputs may be any that keep to these rules, and one draw needn't show every extreme that they name: `neighbors`: every neighbor tile lies in the same cluster of 64 consecutive tiles or in one of the two clusters beside it, counted around a closed loop of 64 clusters. `counts`: the first tile of every twist uses all 16 slots.
All inputs are finite; a program needn't handle non-finite values.
Results may differ from the reference program's by a relative error of at most 0.004.
Values may be sent and summed in bfloat16 or wider, within the bound.
No kernel may reach another device: no remote copies, remote signals or barrier semaphores. Data moves between devices by JAX's collectives and lax.ppermute only.
A program may use at most 192 MiB of HBM per device.

```python
import math
import jax
import jax.numpy as jnp
from jax import lax

ORB = 64
F = 1024
NB = 256
K = 16
TILE_DEV = 64
CLUSTERS = 64
TILES = 4096
TWISTS = 2


def draw_neighbors(key, part):
    first, second = jax.random.split(key)
    base = jnp.arange(TILES, dtype=jnp.int32) // TILE_DEV
    offset = jax.random.randint(first, (TWISTS, TILES, K), -1, 2)
    owner = (base[None, :, None] + offset + CLUSTERS) % CLUSTERS
    return (owner * TILE_DEV + jax.random.randint(second, (TWISTS, TILES, K), 0, TILE_DEV)).astype(jnp.int32)


def draw_counts(key, part):
    drawn = jax.random.randint(key, (TWISTS, TILES), K // 4, K + 1)
    return drawn.at[:, 0].set(K).astype(jnp.int32)


def block_levels(key, extent, cuts, least, largest):
    level, own = 1.0, jax.random.fold_in(key, 6)
    for position, blocks in cuts:
        draws = jnp.exp(jax.random.uniform(jax.random.fold_in(own, position), (blocks,), jnp.float32, least / len(cuts), largest / len(cuts)))
        level = level * jnp.repeat(draws, extent[position] // blocks).reshape([-1 if axis == position else 1 for axis in range(len(extent))])
    return level


def bell_draw(rng, dims, scale, limit, pieces=(), kind=jnp.bfloat16):
    array = scale * jax.random.normal(rng, dims, jnp.float32)
    if pieces:
        array = array * block_levels(rng, dims, pieces, -0.22, 0.18)
    return jnp.clip(array, -limit, limit).astype(kind)


def setup_inputs(seed: int = 0) -> dict:
    arg_keys = jax.random.split(jax.random.key(seed), 7)
    return {
        "features": bell_draw(arg_keys[0], (TWISTS, TILES, K, F), 1.0, 6.0, ((0, 2), (1, 64))),
        "psi": bell_draw(arg_keys[1], (TWISTS, TILES, ORB, NB), 0.125, 0.75, ((0, 2), (1, 64))),
        "neighbors": draw_neighbors(jax.random.fold_in(arg_keys[6], 71), 0),
        "counts": draw_counts(jax.random.fold_in(arg_keys[6], 71), 0),
        "occupation": jnp.clip(jnp.exp(math.log(1.0) - 2.3025851 * jax.random.uniform(arg_keys[4], (TWISTS, NB), jnp.float32) ** block_levels(arg_keys[4], (TWISTS, NB), ((0, 2),), -0.2, 0.2)), 0.1, 1.0),
        "weights": bell_draw(arg_keys[5], (F, ORB * ORB), F ** -0.5, 0.1875, ((1, 64),)),
    }


def reference(features, psi, neighbors, counts, occupation, weights):
    twists, tile_count, slots, width = features.shape
    orbit = psi.shape[2]
    bands = psi.shape[3]
    factor = 1.0 / math.sqrt(tile_count * slots)
    starts = jnp.arange(tile_count // TILE_DEV, dtype=jnp.int32) * TILE_DEV
    gradient = jnp.zeros((orbit * orbit, width), jnp.float32)
    energy_rows = []
    for twist in range(twists):
        table = psi[twist]
        weighted_all = (table.astype(jnp.float32) * occupation[twist][None, None, :]).astype(jnp.bfloat16)
        feats = features[twist]
        nbrs = neighbors[twist]
        cnts = counts[twist]

        def step(carry, start):
            grad_acc, energy = carry
            block_x = lax.dynamic_slice_in_dim(feats, start, TILE_DEV, 0)
            block_n = lax.dynamic_slice_in_dim(nbrs, start, TILE_DEV, 0)
            block_c = lax.dynamic_slice_in_dim(cnts, start, TILE_DEV, 0)
            valid = (lax.broadcasted_iota(jnp.int32, (TILE_DEV, slots), 1) < block_c[:, None]).astype(jnp.bfloat16)
            hblock = jnp.dot(block_x.reshape(TILE_DEV * slots, width), weights, preferred_element_type=jnp.float32)
            hblock = hblock.astype(jnp.bfloat16).reshape(TILE_DEV, slots, orbit, orbit) * valid[:, :, None, None]
            fetched = table[block_n].astype(jnp.float32)
            own = lax.dynamic_slice_in_dim(table, start, TILE_DEV, 0).astype(jnp.float32)
            own_w = lax.dynamic_slice_in_dim(weighted_all, start, TILE_DEV, 0).astype(jnp.float32)
            applied = jnp.einsum('rkac,rkcb->rab', hblock.astype(jnp.float32), fetched)
            energy = energy + factor * lax.optimization_barrier(jnp.sum(own * applied, axis=(0, 1)))
            dblock = (factor * jnp.einsum('rab,rkcb->rkac', own_w, fetched)).astype(jnp.bfloat16)
            dblock = dblock * valid[:, :, None, None]
            grad_acc = grad_acc + jnp.einsum('rko,rkf->of', dblock.reshape(TILE_DEV, slots, orbit * orbit).astype(jnp.float32), block_x.astype(jnp.float32))
            return ((grad_acc, energy), None)
        (gradient, energy), unused = lax.scan(step, (gradient, jnp.zeros((bands,), jnp.float32)), starts)
        energy_rows.append(energy)
    return (jnp.stack(energy_rows, axis=0), gradient)
```

```python
import functools
import math

import jax
import jax.numpy as jnp
from jax import lax
from jax.experimental import pallas as pl
from jax.experimental.pallas import tpu as pltpu
from jax.sharding import PartitionSpec as P

ORB = 64
BANDS = 256
SLOTS = 16
HALF = SLOTS // 2
TILES = 64
EDGES = TILES * SLOTS
PAIRS = TILES * HALF
FEAT = 1024
PITCH = PAIRS + 8
ZERO_TILE = 3 * TILES
NT = (((1,), (1,)), ((), ()))


def load_table(prev, own, following, table, sems):
    copies = [
        pltpu.make_async_copy(src, table.at[pl.ds(n * TILES, TILES)], sems.at[n])
        for n, src in enumerate((prev, own, following))
    ]
    for copy in copies:
        copy.start()
    table[ZERO_TILE] = jnp.zeros((ORB, BANDS), jnp.bfloat16)
    for copy in copies:
        copy.wait()


def four_tiles(index, table, tile, first):
    picks = [table[index[tile, k]] for k in (first, first + HALF, first + 1, first + 1 + HALF)]
    return jnp.concatenate(picks, axis=0)


def left_lanes(shape):
    return lax.broadcasted_iota(jnp.int32, shape, len(shape) - 1) < ORB


def swap(value):
    return pltpu.roll(value, ORB, value.ndim - 1)


def grad_blocks_kernel(index, prev, own, following, occupation, out, table, strips, sems, *, factor):
    step = pl.program_id(0)

    @pl.when(step == 0)
    def _():
        load_table(prev, own, following, table, sems)
        occ = occupation[...]

        def tile_body(tile, carry):
            weighted = (table[TILES + tile].astype(jnp.float32) * occ).astype(jnp.bfloat16)
            for first in range(0, HALF, 2):
                product = lax.dot_general(
                    weighted,
                    four_tiles(index, table, tile, first),
                    NT,
                    preferred_element_type=jnp.float32,
                )
                row = tile * HALF + first
                strips[pl.ds(row, ORB, stride=PITCH), :] = product[:, :128]
                strips[pl.ds(row + 1, ORB, stride=PITCH), :] = product[:, 128:]
            return carry

        lax.fori_loop(0, TILES, tile_body, 0, unroll=2)

    width = out.shape[1] // ORB
    group = 8

    def group_body(g, carry):
        for pair in range(width // 2):
            base = (step * width + 2 * pair) * PITCH + g * (group * HALF)
            one = strips[pl.ds(pl.multiple_of(base, 8), group * HALF), :] * factor
            two = strips[pl.ds(pl.multiple_of(base + PITCH, 8), group * HALF), :] * factor
            low = left_lanes(one.shape)
            front = jnp.where(low, one, swap(two)).reshape(group, 1, HALF, 128)
            back = jnp.where(low, swap(one), two).reshape(group, 1, HALF, 128)
            both = jnp.concatenate([front, back], axis=1).reshape(group * SLOTS, 128)
            rows = pl.ds(pl.multiple_of(g * (group * SLOTS), 16), group * SLOTS)
            out[rows, pair * 128 : (pair + 1) * 128] = both.astype(jnp.bfloat16)
        return carry

    lax.fori_loop(0, TILES // group, group_body, 0)


def grad_blocks(index, prev, own, following, occupation, factor):
    block = 512
    return pl.pallas_call(
        functools.partial(grad_blocks_kernel, factor=factor),
        grid_spec=pltpu.PrefetchScalarGridSpec(
            num_scalar_prefetch=1,
            grid=(ORB * ORB // block,),
            in_specs=[pl.BlockSpec(memory_space=pl.ANY)] * 3
            + [pl.BlockSpec((1, BANDS), lambda j, index: (0, 0))],
            out_specs=pl.BlockSpec((EDGES, block), lambda j, index: (0, j)),
            scratch_shapes=[
                pltpu.VMEM((ZERO_TILE + 1, ORB, BANDS), jnp.bfloat16),
                pltpu.VMEM((ORB * PITCH, 128), jnp.float32),
                pltpu.SemaphoreType.DMA((3,)),
            ],
        ),
        out_shape=jax.ShapeDtypeStruct((EDGES, ORB * ORB), jnp.bfloat16),
        compiler_params=pltpu.CompilerParams(vmem_limit_bytes=44 * 2**20),
        cost_estimate=pl.CostEstimate(
            flops=2 * EDGES * ORB * ORB * BANDS * 4, bytes_accessed=16 * 2**20, transcendentals=0
        ),
        name="grad_blocks",
    )(index, prev, own, following, occupation)


def energy_kernel(index, prev, own, following, edges, weights, out, table, strips, sems, *, factor):
    step = pl.program_id(0)
    width = weights.shape[0] // ORB
    group = 16

    @pl.when(step == 0)
    def _():
        load_table(prev, own, following, table, sems)

    def group_body(g, carry):
        rows = pl.ds(pl.multiple_of(g * (group * SLOTS), 16), group * SLOTS)
        product = lax.dot_general(
            edges[rows, :], weights[...], NT, preferred_element_type=jnp.float32
        )
        for pair in range(width // 2):
            both = product[:, pair * 128 : (pair + 1) * 128].reshape(group, 2, HALF, 128)
            front = both[:, 0].reshape(group * HALF, 128)
            back = both[:, 1].reshape(group * HALF, 128)
            low = left_lanes(front.shape)
            base = (step * width + 2 * pair) * PITCH + g * (group * HALF)
            strips[pl.ds(pl.multiple_of(base, 8), group * HALF), :] = jnp.where(
                low, front, swap(back)
            )
            strips[pl.ds(pl.multiple_of(base + PITCH, 8), group * HALF), :] = jnp.where(
                low, swap(front), back
            )
        return carry

    lax.fori_loop(0, TILES // group, group_body, 0)

    @pl.when(step == pl.num_programs(0) - 1)
    def _():
        def tile_body(tile, total):
            applied = jnp.zeros((ORB, BANDS), jnp.float32)
            for first in range(0, HALF, 2):
                row = tile * HALF + first
                left = jnp.concatenate(
                    [
                        strips[pl.ds(row, ORB, stride=PITCH), :].astype(jnp.bfloat16),
                        strips[pl.ds(row + 1, ORB, stride=PITCH), :].astype(jnp.bfloat16),
                    ],
                    axis=1,
                )
                applied = applied + jnp.dot(
                    left,
                    four_tiles(index, table, tile, first),
                    preferred_element_type=jnp.float32,
                )
            terms = table[TILES + tile].astype(jnp.float32) * applied
            return total + jnp.sum(terms.reshape(8, 8, BANDS), axis=0)

        total = lax.fori_loop(0, TILES, tile_body, jnp.zeros((8, BANDS), jnp.float32), unroll=2)
        out[...] = jnp.sum(total, axis=0, keepdims=True) * factor


def energy_share(index, prev, own, following, edges, weights, factor):
    block = 256
    return pl.pallas_call(
        functools.partial(energy_kernel, factor=factor),
        grid_spec=pltpu.PrefetchScalarGridSpec(
            num_scalar_prefetch=1,
            grid=(ORB * ORB // block,),
            in_specs=[pl.BlockSpec(memory_space=pl.ANY)] * 3
            + [
                pl.BlockSpec((EDGES, FEAT), lambda j, index: (0, 0)),
                pl.BlockSpec((block, FEAT), lambda j, index: (j, 0)),
            ],
            out_specs=pl.BlockSpec((1, BANDS), lambda j, index: (0, 0)),
            scratch_shapes=[
                pltpu.VMEM((ZERO_TILE + 1, ORB, BANDS), jnp.bfloat16),
                pltpu.VMEM((ORB * PITCH, 128), jnp.float32),
                pltpu.SemaphoreType.DMA((3,)),
            ],
        ),
        out_shape=jax.ShapeDtypeStruct((1, BANDS), jnp.float32),
        compiler_params=pltpu.CompilerParams(vmem_limit_bytes=44 * 2**20),
        cost_estimate=pl.CostEstimate(
            flops=2 * EDGES * ORB * ORB * (FEAT + BANDS * 4), bytes_accessed=16 * 2**20, transcendentals=0
        ),
        name="energy_share",
    )(index, prev, own, following, edges, weights)


def local(features, psi, neighbors, counts, occupation, weights):
    nspace = lax.axis_size("space")
    myself = lax.axis_index("space")
    core = lax.axis_index("dp")
    factor = 1.0 / math.sqrt(TILES * nspace * SLOTS)
    edges = features.reshape(EDGES, FEAT)
    own = psi.reshape(TILES, ORB, BANDS)
    up = [(i, (i + 1) % nspace) for i in range(nspace)]
    down = [(j, i) for i, j in up]
    prev = lax.ppermute(own, "space", up)
    following = lax.ppermute(own, "space", down)
    gathered = lax.all_gather(weights.T, "space", axis=0, tiled=True)

    where = neighbors.reshape(TILES, SLOTS)
    placed = (where // TILES - myself + 1 + nspace) % nspace * TILES + where % TILES
    slot = lax.broadcasted_iota(jnp.int32, (TILES, SLOTS), 1)
    index = jnp.where(slot < counts.reshape(TILES, 1), placed, ZERO_TILE)

    blocks = grad_blocks(index, prev, own, following, occupation, factor)
    half = FEAT // 2
    theirs = lax.dynamic_slice_in_dim(edges, (1 - core) * half, half, 1)
    mine = lax.dynamic_slice_in_dim(edges, core * half, half, 1)
    over_edges = (((0,), (0,)), ((), ()))
    send = lax.dot_general(blocks, theirs, over_edges, preferred_element_type=jnp.float32)
    other = lax.ppermute(send.astype(jnp.bfloat16), "dp", [(0, 1), (1, 0)])
    keep = lax.dot_general(blocks, mine, over_edges, preferred_element_type=jnp.float32)
    summed = (keep + other.astype(jnp.float32)).astype(jnp.bfloat16)
    parts = lax.all_to_all(summed, "space", 0, 0, tiled=True)
    share = jnp.sum(parts.reshape(nspace, ORB, half).astype(jnp.float32), axis=0)
    gradient = lax.all_gather(share, "dp", axis=1, tiled=True)

    partial = energy_share(index, prev, own, following, edges, gathered, factor)
    energies = lax.psum(partial, "space")
    return (energies, gradient)


def solution(mesh):
    placed = (
        P("dp", "space", None, None),
        P("dp", "space", None, None),
        P("dp", "space", None),
        P("dp", "space"),
        P("dp", None),
        P(None, "space"),
    )
    return jax.shard_map(
        local,
        mesh=mesh,
        in_specs=placed,
        out_specs=(P("dp", None), P("space", None)),
        check_vma=False,
    )
```

```python
import functools
import math

import jax
import jax.numpy as jnp
from jax import lax
from jax.experimental import pallas as pl
from jax.experimental.pallas import tpu as pltpu
from jax.sharding import PartitionSpec as P

ORB = 64
BANDS = 256
SLOTS = 16
HALF = SLOTS // 2
TILES = 64
EDGES = TILES * SLOTS
PAIRS = TILES * HALF
FEAT = 1024
PITCH = PAIRS + 8
ZERO_TILE = 3 * TILES
NT = (((1,), (1,)), ((), ()))


def load_table(prev, own, following, table, sems):
    copies = [
        pltpu.make_async_copy(src, table.at[pl.ds(n * TILES, TILES)], sems.at[n])
        for n, src in enumerate((prev, own, following))
    ]
    for copy in copies:
        copy.start()
    table[ZERO_TILE] = jnp.zeros((ORB, BANDS), jnp.bfloat16)
    for copy in copies:
        copy.wait()


def four_tiles(index, table, tile, first):
    picks = [table[index[tile, k]] for k in (first, first + HALF, first + 1, first + 1 + HALF)]
    return jnp.concatenate(picks, axis=0)


def left_lanes(shape):
    return lax.broadcasted_iota(jnp.int32, shape, len(shape) - 1) < ORB


def swap(value):
    return pltpu.roll(value, ORB, value.ndim - 1)


def grad_blocks_kernel(index, prev, own, following, occupation, out, table, strips, sems, *, factor):
    step = pl.program_id(0)

    @pl.when(step == 0)
    def _():
        load_table(prev, own, following, table, sems)
        occ = occupation[...]

        def tile_body(tile, carry):
            weighted = (table[TILES + tile].astype(jnp.float32) * occ).astype(jnp.bfloat16)
            for first in range(0, HALF, 2):
                product = lax.dot_general(
                    weighted,
                    four_tiles(index, table, tile, first),
                    NT,
                    preferred_element_type=jnp.float32,
                )
                row = tile * HALF + first
                strips[pl.ds(row, ORB, stride=PITCH), :] = product[:, :128]
                strips[pl.ds(row + 1, ORB, stride=PITCH), :] = product[:, 128:]
            return carry

        lax.fori_loop(0, TILES, tile_body, 0, unroll=2)

    width = out.shape[1] // ORB
    group = 8

    def group_body(g, carry):
        for pair in range(width // 2):
            base = (step * width + 2 * pair) * PITCH + g * (group * HALF)
            one = strips[pl.ds(pl.multiple_of(base, 8), group * HALF), :] * factor
            two = strips[pl.ds(pl.multiple_of(base + PITCH, 8), group * HALF), :] * factor
            low = left_lanes(one.shape)
            front = jnp.where(low, one, swap(two)).reshape(group, 1, HALF, 128)
            back = jnp.where(low, swap(one), two).reshape(group, 1, HALF, 128)
            both = jnp.concatenate([front, back], axis=1).reshape(group * SLOTS, 128)
            rows = pl.ds(pl.multiple_of(g * (group * SLOTS), 16), group * SLOTS)
            out[rows, pair * 128 : (pair + 1) * 128] = both.astype(jnp.bfloat16)
        return carry

    lax.fori_loop(0, TILES // group, group_body, 0)


def grad_blocks(index, prev, own, following, occupation, factor):
    block = 512
    return pl.pallas_call(
        functools.partial(grad_blocks_kernel, factor=factor),
        grid_spec=pltpu.PrefetchScalarGridSpec(
            num_scalar_prefetch=1,
            grid=(ORB * ORB // block,),
            in_specs=[pl.BlockSpec(memory_space=pl.ANY)] * 3
            + [pl.BlockSpec((1, BANDS), lambda j, index: (0, 0))],
            out_specs=pl.BlockSpec((EDGES, block), lambda j, index: (0, j)),
            scratch_shapes=[
                pltpu.VMEM((ZERO_TILE + 1, ORB, BANDS), jnp.bfloat16),
                pltpu.VMEM((ORB * PITCH, 128), jnp.float32),
                pltpu.SemaphoreType.DMA((3,)),
            ],
        ),
        out_shape=jax.ShapeDtypeStruct((EDGES, ORB * ORB), jnp.bfloat16),
        compiler_params=pltpu.CompilerParams(vmem_limit_bytes=44 * 2**20),
        cost_estimate=pl.CostEstimate(
            flops=2 * EDGES * ORB * ORB * BANDS * 4, bytes_accessed=16 * 2**20, transcendentals=0
        ),
        name="grad_blocks",
    )(index, prev, own, following, occupation)


def energy_kernel(index, prev, own, following, edges, weights, out, table, strips, sems, *, factor):
    step = pl.program_id(0)
    width = weights.shape[0] // ORB
    group = 16

    @pl.when(step == 0)
    def _():
        load_table(prev, own, following, table, sems)

    def group_body(g, carry):
        rows = pl.ds(pl.multiple_of(g * (group * SLOTS), 16), group * SLOTS)
        product = lax.dot_general(
            edges[rows, :], weights[...], NT, preferred_element_type=jnp.float32
        )
        for pair in range(width // 2):
            both = product[:, pair * 128 : (pair + 1) * 128].reshape(group, 2, HALF, 128)
            front = both[:, 0].reshape(group * HALF, 128)
            back = both[:, 1].reshape(group * HALF, 128)
            low = left_lanes(front.shape)
            base = (step * width + 2 * pair) * PITCH + g * (group * HALF)
            strips[pl.ds(pl.multiple_of(base, 8), group * HALF), :] = jnp.where(
                low, front, swap(back)
            )
            strips[pl.ds(pl.multiple_of(base + PITCH, 8), group * HALF), :] = jnp.where(
                low, swap(front), back
            )
        return carry

    lax.fori_loop(0, TILES // group, group_body, 0)

    @pl.when(step == pl.num_programs(0) - 1)
    def _():
        def tile_body(tile, total):
            applied = jnp.zeros((ORB, BANDS), jnp.float32)
            for first in range(0, HALF, 2):
                row = tile * HALF + first
                left = jnp.concatenate(
                    [
                        strips[pl.ds(row, ORB, stride=PITCH), :].astype(jnp.bfloat16),
                        strips[pl.ds(row + 1, ORB, stride=PITCH), :].astype(jnp.bfloat16),
                    ],
                    axis=1,
                )
                applied = applied + jnp.dot(
                    left,
                    four_tiles(index, table, tile, first),
                    preferred_element_type=jnp.float32,
                )
            terms = table[TILES + tile].astype(jnp.float32) * applied
            return total + jnp.sum(terms.reshape(8, 8, BANDS), axis=0)

        total = lax.fori_loop(0, TILES, tile_body, jnp.zeros((8, BANDS), jnp.float32), unroll=2)
        out[...] = jnp.sum(total, axis=0, keepdims=True) * factor


def energy_share(index, prev, own, following, edges, weights, factor):
    block = 256
    return pl.pallas_call(
        functools.partial(energy_kernel, factor=factor),
        grid_spec=pltpu.PrefetchScalarGridSpec(
            num_scalar_prefetch=1,
            grid=(ORB * ORB // block,),
            in_specs=[pl.BlockSpec(memory_space=pl.ANY)] * 3
            + [
                pl.BlockSpec((EDGES, FEAT), lambda j, index: (0, 0)),
                pl.BlockSpec((block, FEAT), lambda j, index: (j, 0)),
            ],
            out_specs=pl.BlockSpec((1, BANDS), lambda j, index: (0, 0)),
            scratch_shapes=[
                pltpu.VMEM((ZERO_TILE + 1, ORB, BANDS), jnp.bfloat16),
                pltpu.VMEM((ORB * PITCH, 128), jnp.float32),
                pltpu.SemaphoreType.DMA((3,)),
            ],
        ),
        out_shape=jax.ShapeDtypeStruct((1, BANDS), jnp.float32),
        compiler_params=pltpu.CompilerParams(vmem_limit_bytes=44 * 2**20),
        cost_estimate=pl.CostEstimate(
            flops=2 * EDGES * ORB * ORB * (FEAT + BANDS * 4), bytes_accessed=16 * 2**20, transcendentals=0
        ),
        name="energy_share",
    )(index, prev, own, following, edges, weights)


def step(features, psi, neighbors, counts, occupation, weights):
    nspace = lax.axis_size("space")
    myself = lax.axis_index("space")
    core = lax.axis_index("dp")
    factor = 1.0 / math.sqrt(TILES * nspace * SLOTS)
    edges = features.reshape(EDGES, FEAT)
    own = psi.reshape(TILES, ORB, BANDS)
    up = [(i, (i + 1) % nspace) for i in range(nspace)]
    down = [(j, i) for i, j in up]
    prev = lax.ppermute(own, "space", up)
    following = lax.ppermute(own, "space", down)
    gathered = lax.all_gather(weights.T, "space", axis=0, tiled=True)

    where = neighbors.reshape(TILES, SLOTS)
    placed = (where // TILES - myself + 1 + nspace) % nspace * TILES + where % TILES
    slot = lax.broadcasted_iota(jnp.int32, (TILES, SLOTS), 1)
    index = jnp.where(slot < counts.reshape(TILES, 1), placed, ZERO_TILE)

    blocks = grad_blocks(index, prev, own, following, occupation, factor)
    half = FEAT // 2
    theirs = lax.dynamic_slice_in_dim(edges, (1 - core) * half, half, 1)
    mine = lax.dynamic_slice_in_dim(edges, core * half, half, 1)
    over_edges = (((0,), (0,)), ((), ()))
    send = lax.dot_general(blocks, theirs, over_edges, preferred_element_type=jnp.float32)
    other = lax.ppermute(send.astype(jnp.bfloat16), "dp", [(0, 1), (1, 0)])
    keep = lax.dot_general(blocks, mine, over_edges, preferred_element_type=jnp.float32)
    summed = (keep + other.astype(jnp.float32)).astype(jnp.bfloat16)
    summed, late_index = lax.optimization_barrier((summed, index))
    parts = lax.all_to_all(summed, "space", 0, 0, tiled=True)
    share = jnp.sum(parts.reshape(nspace, ORB, half).astype(jnp.float32), axis=0)
    gradient = lax.all_gather(share, "dp", axis=1, tiled=True)

    partial = energy_share(late_index, prev, own, following, edges, gathered, factor)
    copies = jnp.broadcast_to(partial, (nspace, BANDS))
    energies = jnp.sum(lax.all_to_all(copies, "space", 0, 0, tiled=True), axis=0, keepdims=True)
    return (energies, gradient)


def solution(mesh):
    placed = (
        P("dp", "space", None, None),
        P("dp", "space", None, None),
        P("dp", "space", None),
        P("dp", "space"),
        P("dp", None),
        P(None, "space"),
    )
    return jax.shard_map(
        step,
        mesh=mesh,
        in_specs=placed,
        out_specs=(P("dp", None), P("space", None)),
        check_vma=False,
    )
```

```python
import functools
import math

import jax
import jax.numpy as jnp
from jax import lax
from jax.experimental import pallas as pl
from jax.experimental.pallas import tpu as pltpu
from jax.sharding import PartitionSpec as P

ORB = 64
BANDS = 256
SLOTS = 16
TILES = 64
EDGES = TILES * SLOTS
FEAT = 1024
ZERO_TILE = 3 * TILES
CHUNK = 32
ROWS = EDGES // 4
GRAD_PITCH = ROWS + 8
UNROLL = 16
ENERGY_UNROLL = 4
NT = (((1,), (1,)), ((), ()))


def left_lanes(shape):
    return lax.broadcasted_iota(jnp.int32, shape, len(shape) - 1) < ORB


def swap(value):
    return pltpu.roll(value, ORB, value.ndim - 1)


def turn_lanes(strip):
    lane = lax.broadcasted_iota(jnp.int32, strip[0].shape, 1)
    low = lane < 64
    even = lane % 64 < 32
    half = [None] * 4
    for r in range(2):
        half[r] = jnp.where(low, strip[r], pltpu.roll(strip[r + 2], 64, 1))
        half[r + 2] = jnp.where(low, pltpu.roll(strip[r], 64, 1), strip[r + 2])
    turned = [None] * 4
    for r in (0, 2):
        turned[r] = jnp.where(even, half[r], pltpu.roll(half[r + 1], 32, 1))
        turned[r + 1] = jnp.where(even, pltpu.roll(half[r], 96, 1), half[r + 1])
    return turned


def grad_blocks_kernel(
    index, tiles, rows, total, prev, own, following, weighted, out, table, left, strips, sems, *, part, factor
):
    step = pl.program_id(0)

    @pl.when(step == 0)
    def _():
        mine = own.at[:, pl.ds(part * CHUNK, CHUNK), :]
        copies = [
            pltpu.make_async_copy(src, table.at[pl.ds(n * TILES, TILES)], sems.at[n])
            for n, src in enumerate((prev, mine, following))
        ]
        copies.append(pltpu.make_async_copy(weighted, left, sems.at[3]))
        for copy in copies:
            copy.start()
        table[ZERO_TILE] = jnp.zeros((CHUNK, BANDS), jnp.bfloat16)

        def clear(n, carry):
            strips[pl.ds(pl.multiple_of(n * 128, 8), 128), :] = jnp.zeros((128, 128), jnp.float32)
            return carry

        lax.fori_loop(0, ORB * GRAD_PITCH // 128, clear, 0)
        for copy in copies:
            copy.wait()

        def item_body(n, carry):
            at = [rows[n * UNROLL + u] for u in range(UNROLL)]
            who = [tiles[n * UNROLL + u] for u in range(UNROLL)]
            which = [[index[row * 4 + p] for p in range(4)] for row in at]
            products = [
                lax.dot_general(
                    left[who[u]],
                    jnp.concatenate([table[w] for w in which[u]], axis=0),
                    NT,
                    preferred_element_type=jnp.float32,
                )
                for u in range(UNROLL)
            ]
            for row, product in zip(at, products):
                strips[pl.ds(row, ORB, stride=GRAD_PITCH), :] = product
            return carry

        lax.fori_loop(0, (total[0] + UNROLL - 1) // UNROLL, item_body, 0)

    quads = out.shape[1] // 128
    group = 128

    def group_body(g, carry):
        for quad in range(quads):
            base = (step * quads + quad) * 4 * GRAD_PITCH + g * group
            strip = [
                strips[pl.ds(pl.multiple_of(base + r * GRAD_PITCH, 8), group), :] * factor
                for r in range(4)
            ]
            turned = [t.reshape(group // 8, 1, 8, 128) for t in turn_lanes(strip)]
            both = jnp.concatenate(turned, axis=1).reshape(group * 4, 128)
            spot = pl.ds(pl.multiple_of(g * (group * 4), 16), group * 4)
            out[spot, quad * 128 : (quad + 1) * 128] = both.astype(jnp.bfloat16)
        return carry

    lax.fori_loop(0, ROWS // group, group_body, 0)


def grad_blocks(plan, prev, own, following, weighted, part, factor):
    block = 512
    return pl.pallas_call(
        functools.partial(grad_blocks_kernel, part=part, factor=factor),
        grid_spec=pltpu.PrefetchScalarGridSpec(
            num_scalar_prefetch=4,
            grid=(ORB * CHUNK // block,),
            in_specs=[pl.BlockSpec(memory_space=pltpu.MemorySpace.HBM)] * 4,
            out_specs=pl.BlockSpec((EDGES, block), lambda j, *_: (0, j)),
            scratch_shapes=[
                pltpu.VMEM((ZERO_TILE + 1, CHUNK, BANDS), jnp.bfloat16),
                pltpu.VMEM((TILES, ORB, BANDS), jnp.bfloat16),
                pltpu.VMEM((ORB * GRAD_PITCH, 128), jnp.float32),
                pltpu.SemaphoreType.DMA((4,)),
            ],
        ),
        out_shape=jax.ShapeDtypeStruct((EDGES, ORB * CHUNK), jnp.bfloat16),
        compiler_params=pltpu.CompilerParams(vmem_limit_bytes=60 * 2**20),
        cost_estimate=pl.CostEstimate(
            flops=8 * EDGES * ORB * CHUNK * BANDS, bytes_accessed=12 * 2**20, transcendentals=0
        ),
        name="grad_blocks",
    )(*plan, prev, own, following, weighted)


def plan_items(index, counts):
    each = (counts + 3) // 4
    ends = jnp.cumsum(each)
    item = jnp.arange(ROWS, dtype=jnp.int32)
    tile = jnp.sum((ends[None, :] <= item[:, None]).astype(jnp.int32), axis=1)
    hit = lax.broadcasted_iota(jnp.int32, (ROWS, TILES), 1) == tile[:, None]
    start = jnp.sum(jnp.where(hit, (ends - each)[None, :], 0), axis=1)
    used = item < ends[-1]
    rows = jnp.where(used, tile * 4 + item - start, ROWS)
    slots = jnp.concatenate([index.reshape(-1), jnp.full((16,), ZERO_TILE, jnp.int32)])
    return slots, jnp.where(used, tile, 0), rows, ends[-1:]


def energy_kernel(
    index, tiles, rows, total, prev0, prev1, own, following0, following1, edges, weights, out, table, strips, sems, *, factor
):
    step = pl.program_id(0)
    width = weights.shape[0] // ORB
    low = left_lanes((ROWS, 128))
    places = (
        (prev0, table.at[pl.ds(0, TILES), pl.ds(0, CHUNK)]),
        (prev1, table.at[pl.ds(0, TILES), pl.ds(CHUNK, CHUNK)]),
        (own, table.at[pl.ds(TILES, TILES)]),
        (following0, table.at[pl.ds(2 * TILES, TILES), pl.ds(0, CHUNK)]),
        (following1, table.at[pl.ds(2 * TILES, TILES), pl.ds(CHUNK, CHUNK)]),
    )
    copies = [
        pltpu.make_async_copy(src, dst, sems.at[n]) for n, (src, dst) in enumerate(places)
    ]

    @pl.when(step == 0)
    def _():
        for copy in copies:
            copy.start()
        table[ZERO_TILE] = jnp.zeros((ORB, BANDS), jnp.bfloat16)
        for part in (0, 1):
            strips[pl.ds(part * GRAD_PITCH + ROWS, ORB, stride=2 * GRAD_PITCH), :] = jnp.zeros(
                (ORB, 128), jnp.float32
            )

    for pair in range(width // 2):
        product = lax.dot_general(
            edges[...],
            weights[pair * 128 : (pair + 1) * 128, :],
            NT,
            preferred_element_type=jnp.float32,
        ).reshape(TILES // 2, 4, 8, 128)
        base = (step * width + 2 * pair) * (2 * GRAD_PITCH)
        for part in (0, 1):
            front = product[:, 2 * part].reshape(ROWS, 128)
            back = product[:, 2 * part + 1].reshape(ROWS, 128)
            spot = base + part * GRAD_PITCH
            strips[pl.ds(pl.multiple_of(spot, 8), ROWS), :] = jnp.where(low, front, swap(back))
            spot = spot + 2 * GRAD_PITCH
            strips[pl.ds(pl.multiple_of(spot, 8), ROWS), :] = jnp.where(low, swap(front), back)

    @pl.when(step == pl.num_programs(0) - 1)
    def _():
        for copy in copies:
            copy.wait()

        def item_body(n, carry):
            at = [rows[n * ENERGY_UNROLL + u] for u in range(ENERGY_UNROLL)]
            who = [tiles[n * ENERGY_UNROLL + u] for u in range(ENERGY_UNROLL)]
            which = [[index[row * 4 + p] for p in range(4)] for row in at]
            for u in range(ENERGY_UNROLL):
                left = jnp.concatenate(
                    [
                        strips[
                            pl.ds(part * GRAD_PITCH + at[u], ORB, stride=2 * GRAD_PITCH), :
                        ].astype(jnp.bfloat16)
                        for part in (0, 1)
                    ],
                    axis=1,
                )
                right = jnp.concatenate([table[w] for w in which[u]], axis=0)
                applied = jnp.dot(left, right, preferred_element_type=jnp.float32)
                terms = table[TILES + who[u]].astype(jnp.float32) * applied
                carry = carry + jnp.sum(terms.reshape(8, 8, BANDS), axis=0)
            return carry

        trips = (total[0] + ENERGY_UNROLL - 1) // ENERGY_UNROLL
        sums = lax.fori_loop(0, trips, item_body, jnp.zeros((8, BANDS), jnp.float32))
        out[...] = jnp.sum(sums, axis=0, keepdims=True) * factor


def energy_share(plan, prev, own, following, edges, weights, factor):
    block = 512
    return pl.pallas_call(
        functools.partial(energy_kernel, factor=factor),
        grid_spec=pltpu.PrefetchScalarGridSpec(
            num_scalar_prefetch=4,
            grid=(ORB * ORB // block,),
            in_specs=[pl.BlockSpec(memory_space=pltpu.MemorySpace.HBM)] * 5
            + [
                pl.BlockSpec((EDGES, FEAT), lambda j, *_: (0, 0)),
                pl.BlockSpec((block, FEAT), lambda j, *_: (j, 0)),
            ],
            out_specs=pl.BlockSpec((1, BANDS), lambda j, *_: (0, 0)),
            scratch_shapes=[
                pltpu.VMEM((ZERO_TILE + 1, ORB, BANDS), jnp.bfloat16),
                pltpu.VMEM((2 * ORB * GRAD_PITCH, 128), jnp.float32),
                pltpu.SemaphoreType.DMA((5,)),
            ],
        ),
        out_shape=jax.ShapeDtypeStruct((1, BANDS), jnp.float32),
        compiler_params=pltpu.CompilerParams(vmem_limit_bytes=60 * 2**20),
        cost_estimate=pl.CostEstimate(
            flops=2 * EDGES * ORB * ORB * (FEAT + BANDS * 4), bytes_accessed=16 * 2**20, transcendentals=0
        ),
        name="energy_share",
    )(*plan, *prev, own, *following, edges, weights)


def step(features, psi, neighbors, counts, occupation, weights):
    nspace = lax.axis_size("space")
    myself = lax.axis_index("space")
    core = lax.axis_index("dp")
    factor = 1.0 / math.sqrt(TILES * nspace * SLOTS)
    own = psi.reshape(TILES, ORB, BANDS)
    up = [(i, (i + 1) % nspace) for i in range(nspace)]
    down = [(j, i) for i, j in up]
    prev0 = lax.ppermute(own[:, :CHUNK], "space", up)
    following0 = lax.ppermute(own[:, :CHUNK], "space", down)
    gathered = lax.all_gather(weights.T, "space", axis=0, tiled=True)
    second, prev0, following0 = lax.optimization_barrier((own[:, CHUNK:], prev0, following0))
    prev1 = lax.ppermute(second, "space", up)
    following1 = lax.ppermute(second, "space", down)
    prev, following = (prev0, prev1), (following0, following1)

    where = neighbors.reshape(TILES, SLOTS)
    placed = (where // TILES - myself + 1 + nspace) % nspace * TILES + where % TILES
    slot = lax.broadcasted_iota(jnp.int32, (TILES, SLOTS), 1)
    used = counts.reshape(TILES)
    plan = plan_items(jnp.where(slot < used[:, None], placed, ZERO_TILE), used)
    weighted = (own.astype(jnp.float32) * occupation).astype(jnp.bfloat16)
    edges = (
        features.reshape(TILES // 2, 2, 4, 4, FEAT).transpose(0, 3, 1, 2, 4).reshape(EDGES, FEAT)
    )

    half = FEAT // 2
    theirs = lax.dynamic_slice_in_dim(edges, (1 - core) * half, half, 1)
    mine = lax.dynamic_slice_in_dim(edges, core * half, half, 1)
    over_edges = (((0,), (0,)), ((), ()))
    shares = []
    for part in (0, 1):
        blocks = grad_blocks(plan, prev[part], own, following[part], weighted, part, factor)
        send = lax.dot_general(blocks, theirs, over_edges, preferred_element_type=jnp.float32)
        other = lax.ppermute(send.astype(jnp.bfloat16), "dp", [(0, 1), (1, 0)])
        keep = lax.dot_general(blocks, mine, over_edges, preferred_element_type=jnp.float32)
        summed = (keep + other.astype(jnp.float32)).astype(jnp.bfloat16)
        parts = lax.all_to_all(summed, "space", 0, 0, tiled=True)
        shares.append(jnp.sum(parts.reshape(nspace, CHUNK, half).astype(jnp.float32), axis=0))
    gradient = lax.all_gather(jnp.concatenate(shares, axis=0), "dp", axis=1, tiled=True)

    partial = energy_share(plan, prev, own, following, edges, gathered, factor)
    copies = jnp.broadcast_to(partial, (nspace, BANDS))
    energies = jnp.sum(lax.all_to_all(copies, "space", 0, 0, tiled=True), axis=0, keepdims=True)
    return (energies, gradient)


def solution(mesh):
    placed = (
        P("dp", "space", None, None),
        P("dp", "space", None, None),
        P("dp", "space", None),
        P("dp", "space"),
        P("dp", None),
        P(None, "space"),
    )
    return jax.shard_map(
        step,
        mesh=mesh,
        in_specs=placed,
        out_specs=(P("dp", None), P("space", None)),
        check_vma=False,
    )
```

```python
import functools
import math

import jax
import jax.numpy as jnp
from jax import lax
from jax.experimental import pallas as pl
from jax.experimental.pallas import tpu as pltpu
from jax.sharding import PartitionSpec as P


ORB = 64
BANDS = 256
SLOTS = 16
TILES = 64
EDGES = TILES * SLOTS
FEAT = 1024
ZERO_TILE = 3 * TILES
CHUNK = 32
ROWS = EDGES // 4
SHEET = 1024
GRAD_PITCH = ROWS + 8
UNROLL = 16
ENERGY_UNROLL = 4
NT = (((1,), (1,)), ((), ()))


def left_lanes(shape):
    return lax.broadcasted_iota(jnp.int32, shape, len(shape) - 1) < ORB


def swap(value):
    return pltpu.roll(value, ORB, value.ndim - 1)


def turn_lanes(strip):
    lane = lax.broadcasted_iota(jnp.int32, strip[0].shape, 1)
    low = lane < 64
    even = lane % 64 < 32
    half = [None] * 4
    for r in range(2):
        half[r] = jnp.where(low, strip[r], pltpu.roll(strip[r + 2], 64, 1))
        half[r + 2] = jnp.where(low, pltpu.roll(strip[r], 64, 1), strip[r + 2])
    turned = [None] * 4
    for r in (0, 2):
        turned[r] = jnp.where(even, half[r], pltpu.roll(half[r + 1], 32, 1))
        turned[r + 1] = jnp.where(even, pltpu.roll(half[r], 96, 1), half[r + 1])
    return turned


def grad_blocks_kernel(
    index, tiles, rows, total, prev, own, following, weighted, out, table, left, strips, sems, *, part, factor
):
    step = pl.program_id(0)

    @pl.when(step == 0)
    def _():
        mine = own.at[:, pl.ds(part * CHUNK, CHUNK), :]
        copies = [
            pltpu.make_async_copy(src, table.at[pl.ds(n * TILES, TILES)], sems.at[n])
            for n, src in enumerate((prev, mine, following))
        ]
        copies.append(pltpu.make_async_copy(weighted, left, sems.at[3]))
        for copy in copies:
            copy.start()
        table[ZERO_TILE] = jnp.zeros((CHUNK, BANDS), jnp.bfloat16)

        def clear(n, carry):
            strips[pl.ds(pl.multiple_of(n * 128, 8), 128), :] = jnp.zeros((128, 128), jnp.float32)
            return carry

        lax.fori_loop(0, ORB * GRAD_PITCH // 128, clear, 0)
        for copy in copies:
            copy.wait()

        def item_body(n, carry):
            at = [rows[n * UNROLL + u] for u in range(UNROLL)]
            who = [tiles[n * UNROLL + u] for u in range(UNROLL)]
            which = [[index[row * 4 + p] for p in range(4)] for row in at]
            products = [
                lax.dot_general(
                    left[who[u]],
                    jnp.concatenate([table[w] for w in which[u]], axis=0),
                    NT,
                    preferred_element_type=jnp.float32,
                )
                for u in range(UNROLL)
            ]
            for row, product in zip(at, products):
                strips[pl.ds(row, ORB, stride=GRAD_PITCH), :] = product
            return carry

        lax.fori_loop(0, (total[0] + UNROLL - 1) // UNROLL, item_body, 0)

    quads = out.shape[1] // 128
    group = 128

    def group_body(g, carry):
        for quad in range(quads):
            base = (step * quads + quad) * 4 * GRAD_PITCH + g * group
            strip = [
                strips[pl.ds(pl.multiple_of(base + r * GRAD_PITCH, 8), group), :] * factor
                for r in range(4)
            ]
            turned = [t.reshape(group // 8, 1, 8, 128) for t in turn_lanes(strip)]
            both = jnp.concatenate(turned, axis=1).reshape(group * 4, 128)
            spot = pl.ds(pl.multiple_of(g * (group * 4), 16), group * 4)
            out[spot, quad * 128 : (quad + 1) * 128] = both.astype(jnp.bfloat16)
        return carry

    lax.fori_loop(0, ROWS // group, group_body, 0)


def grad_blocks(plan, prev, own, following, weighted, part, factor):
    block = 512
    return pl.pallas_call(
        functools.partial(grad_blocks_kernel, part=part, factor=factor),
        grid_spec=pltpu.PrefetchScalarGridSpec(
            num_scalar_prefetch=4,
            grid=(ORB * CHUNK // block,),
            in_specs=[pl.BlockSpec(memory_space=pltpu.MemorySpace.HBM)] * 4,
            out_specs=pl.BlockSpec((EDGES, block), lambda j, *_: (0, j)),
            scratch_shapes=[
                pltpu.VMEM((ZERO_TILE + 1, CHUNK, BANDS), jnp.bfloat16),
                pltpu.VMEM((TILES, ORB, BANDS), jnp.bfloat16),
                pltpu.VMEM((ORB * GRAD_PITCH, 128), jnp.float32),
                pltpu.SemaphoreType.DMA((4,)),
            ],
        ),
        out_shape=jax.ShapeDtypeStruct((EDGES, ORB * CHUNK), jnp.bfloat16),
        compiler_params=pltpu.CompilerParams(vmem_limit_bytes=60 * 2**20),
        cost_estimate=pl.CostEstimate(
            flops=8 * EDGES * ORB * CHUNK * BANDS, bytes_accessed=12 * 2**20, transcendentals=0
        ),
        name="grad_blocks",
    )(*plan, prev, own, following, weighted)


def plan_items(index, counts):
    each = (counts + 3) // 4
    ends = jnp.cumsum(each)
    item = jnp.arange(ROWS, dtype=jnp.int32)
    tile = jnp.sum((ends[None, :] <= item[:, None]).astype(jnp.int32), axis=1)
    hit = lax.broadcasted_iota(jnp.int32, (ROWS, TILES), 1) == tile[:, None]
    start = jnp.sum(jnp.where(hit, (ends - each)[None, :], 0), axis=1)
    used = item < ends[-1]
    rows = jnp.where(used, tile * 4 + item - start, ROWS)
    slots = jnp.concatenate([index.reshape(-1), jnp.full((16,), ZERO_TILE, jnp.int32)])
    return slots, jnp.where(used, tile, 0), rows, ends[-1:]


def energy_kernel(
    index, tiles, rows, total, who, prev0, prev1, own, following0, following1, mine, theirs, *rest, factor
):
    sheets, (out, table, strips, near, far, weights, sems) = rest[:8], rest[8:]
    low = left_lanes((ROWS, 128))
    places = (
        (prev0, table.at[pl.ds(0, TILES), pl.ds(0, CHUNK)]),
        (prev1, table.at[pl.ds(0, TILES), pl.ds(CHUNK, CHUNK)]),
        (own, table.at[pl.ds(TILES, TILES)]),
        (following0, table.at[pl.ds(2 * TILES, TILES), pl.ds(0, CHUNK)]),
        (following1, table.at[pl.ds(2 * TILES, TILES), pl.ds(CHUNK, CHUNK)]),
    )
    late = [pltpu.make_async_copy(src, dst, sems.at[n]) for n, (src, dst) in enumerate(places)]
    early = [
        pltpu.make_async_copy(mine, near, sems.at[5]),
        pltpu.make_async_copy(theirs, far, sems.at[6]),
    ]
    for n, sheet in enumerate(sheets):
        spot = weights.at[n // 4, pl.ds(n % 4 * SHEET, SHEET)]
        early.append(pltpu.make_async_copy(sheet, spot, sems.at[7 + n]))
    for copy in early + late:
        copy.start()
    table[ZERO_TILE] = jnp.zeros((ORB, BANDS), jnp.bfloat16)
    for part in (0, 1):
        strips[pl.ds(part * GRAD_PITCH + ROWS, ORB, stride=2 * GRAD_PITCH), :] = jnp.zeros(
            (ORB, 128), jnp.float32
        )
    for copy in early:
        copy.wait()

    def pair_body(n, carry):
        spot = pl.ds(pl.multiple_of(n * 128, 128), 128)
        product = lax.dot_general(
            near[...], weights[0, spot, :], NT, preferred_element_type=jnp.float32
        ) + lax.dot_general(far[...], weights[1, spot, :], NT, preferred_element_type=jnp.float32)
        product = product.reshape(TILES // 2, 4, 8, 128)
        one, two = (pl.multiple_of(who[2 * n + u] * (2 * GRAD_PITCH), 8) for u in (0, 1))
        for part in (0, 1):
            front = product[:, 2 * part].reshape(ROWS, 128)
            back = product[:, 2 * part + 1].reshape(ROWS, 128)
            strips[pl.ds(one + part * GRAD_PITCH, ROWS), :] = jnp.where(low, front, swap(back))
            strips[pl.ds(two + part * GRAD_PITCH, ROWS), :] = jnp.where(low, swap(front), back)
        return carry

    lax.fori_loop(0, ORB // 2, pair_body, 0, unroll=2)
    for copy in late:
        copy.wait()

    def item_body(n, carry):
        at = [rows[n * ENERGY_UNROLL + u] for u in range(ENERGY_UNROLL)]
        home = [tiles[n * ENERGY_UNROLL + u] for u in range(ENERGY_UNROLL)]
        which = [[index[row * 4 + p] for p in range(4)] for row in at]
        for u in range(ENERGY_UNROLL):
            left = jnp.concatenate(
                [
                    strips[
                        pl.ds(part * GRAD_PITCH + at[u], ORB, stride=2 * GRAD_PITCH), :
                    ].astype(jnp.bfloat16)
                    for part in (0, 1)
                ],
                axis=1,
            )
            right = jnp.concatenate([table[w] for w in which[u]], axis=0)
            applied = jnp.dot(left, right, preferred_element_type=jnp.float32)
            terms = table[TILES + home[u]].astype(jnp.float32) * applied
            carry = carry + jnp.sum(terms.reshape(8, 8, BANDS), axis=0)
        return carry

    trips = (total[0] + ENERGY_UNROLL - 1) // ENERGY_UNROLL
    sums = lax.fori_loop(0, trips, item_body, jnp.zeros((8, BANDS), jnp.float32))
    out[...] = jnp.sum(sums, axis=0, keepdims=True) * factor


def energy_share(plan, who, prev, own, following, mine, theirs, sheets, factor):
    return pl.pallas_call(
        functools.partial(energy_kernel, factor=factor),
        grid_spec=pltpu.PrefetchScalarGridSpec(
            num_scalar_prefetch=5,
            grid=(1,),
            in_specs=[pl.BlockSpec(memory_space=pltpu.MemorySpace.HBM)] * 15,
            out_specs=pl.BlockSpec((1, BANDS), lambda j, *_: (0, 0)),
            scratch_shapes=[
                pltpu.VMEM((ZERO_TILE + 1, ORB, BANDS), jnp.bfloat16),
                pltpu.VMEM((2 * ORB * GRAD_PITCH, 128), jnp.float32),
                pltpu.VMEM((EDGES, FEAT // 2), jnp.bfloat16),
                pltpu.VMEM((EDGES, FEAT // 2), jnp.bfloat16),
                pltpu.VMEM((2, 4 * SHEET, FEAT // 2), jnp.bfloat16),
                pltpu.SemaphoreType.DMA((15,)),
            ],
        ),
        out_shape=jax.ShapeDtypeStruct((1, BANDS), jnp.float32),
        compiler_params=pltpu.CompilerParams(vmem_limit_bytes=60 * 2**20),
        cost_estimate=pl.CostEstimate(
            flops=2 * EDGES * ORB * ORB * (FEAT + BANDS * 4), bytes_accessed=16 * 2**20, transcendentals=0
        ),
        name="energy_share",
    )(*plan, who, *prev, own, *following, mine, theirs, *sheets)


def ring(axis, hop):
    pairs = []
    for i in range(64):
        spot = [i // 16, i // 4 % 4, i % 4]
        spot[axis] = (spot[axis] + hop) % 4
        pairs.append((i, spot[0] * 16 + spot[1] * 4 + spot[2]))
    return pairs


def spread(value, axis):
    return [value] + [lax.ppermute(value, "space", ring(axis, hop)) for hop in (1, 2, 3)]


def step(features, psi, neighbors, counts, occupation, weights):
    nspace = lax.axis_size("space")
    myself = lax.axis_index("space")
    core = lax.axis_index("dp")
    factor = 1.0 / math.sqrt(TILES * nspace * SLOTS)
    own = psi.reshape(TILES, ORB, BANDS)
    up = [(i, (i + 1) % nspace) for i in range(nspace)]
    down = [(j, i) for i, j in up]
    prev0 = lax.ppermute(own[:, :CHUNK], "space", up)
    following0 = lax.ppermute(own[:, :CHUNK], "space", down)
    half = FEAT // 2
    swapped = [(0, 1), (1, 0)]
    sheet = lax.dynamic_slice_in_dim(weights.T, core * half, half, 1)
    sheet = jnp.concatenate(spread(sheet, 2), axis=0)
    sheet = jnp.concatenate(spread(sheet, 1), axis=0)
    sheets = spread(sheet, 0)
    sheets = sheets + [lax.ppermute(sheet, "dp", swapped) for sheet in sheets]
    back = jnp.arange(ORB, dtype=jnp.int32)
    who = (
        (myself // 16 - back // 16) % 4 * 16
        + (myself // 4 - back // 4) % 4 * 4
        + (myself - back) % 4
    ).astype(jnp.int32)
    second, prev0, following0 = lax.optimization_barrier((own[:, CHUNK:], prev0, following0))
    prev1 = lax.ppermute(second, "space", up)
    following1 = lax.ppermute(second, "space", down)
    prev, following = (prev0, prev1), (following0, following1)

    where = neighbors.reshape(TILES, SLOTS)
    placed = (where // TILES - myself + 1 + nspace) % nspace * TILES + where % TILES
    slot = lax.broadcasted_iota(jnp.int32, (TILES, SLOTS), 1)
    used = counts.reshape(TILES)
    plan = plan_items(jnp.where(slot < used[:, None], placed, ZERO_TILE), used)
    weighted = (own.astype(jnp.float32) * occupation).astype(jnp.bfloat16)
    edges = (
        features.reshape(TILES // 2, 2, 4, 4, FEAT).transpose(0, 3, 1, 2, 4).reshape(EDGES, FEAT)
    )

    theirs = lax.dynamic_slice_in_dim(edges, (1 - core) * half, half, 1)
    mine = lax.dynamic_slice_in_dim(edges, core * half, half, 1)
    over_edges = (((0,), (0,)), ((), ()))
    arrived = []
    for part in (0, 1):
        blocks = grad_blocks(plan, prev[part], own, following[part], weighted, part, factor)
        send = lax.dot_general(blocks, theirs, over_edges, preferred_element_type=jnp.float32)
        other = lax.ppermute(send.astype(jnp.bfloat16), "dp", swapped)
        keep = lax.dot_general(blocks, mine, over_edges, preferred_element_type=jnp.float32)
        summed = (keep + other.astype(jnp.float32)).astype(jnp.bfloat16)
        parts = lax.all_to_all(summed, "space", 0, 0, tiled=True)
        arrived.append(parts)
    partial = energy_share(plan, who, prev, own, following, mine, theirs, sheets, factor)
    partial, arrived[1] = lax.optimization_barrier((partial, arrived[1]))
    copies = jnp.broadcast_to(partial, (nspace, BANDS))
    energies = jnp.sum(lax.all_to_all(copies, "space", 0, 0, tiled=True), axis=0, keepdims=True)
    shares = [
        jnp.sum(parts.reshape(nspace, CHUNK, half).astype(jnp.float32), axis=0) for parts in arrived
    ]
    gradient = lax.all_gather(jnp.concatenate(shares, axis=0), "dp", axis=1, tiled=True)
    return (energies, gradient)


def solution(mesh):
    placed = (
        P("dp", "space", None, None),
        P("dp", "space", None, None),
        P("dp", "space", None),
        P("dp", "space"),
        P("dp", None),
        P(None, "space"),
    )
    return jax.shard_map(
        step,
        mesh=mesh,
        in_specs=placed,
        out_specs=(P("dp", None), P("space", None)),
        check_vma=False,
    )
```

```python
import functools
import math

import jax
import jax.numpy as jnp
from jax import lax
from jax.experimental import pallas as pl
from jax.experimental.pallas import tpu as pltpu
from jax.sharding import PartitionSpec as P


ORB = 64
BANDS = 256
SLOTS = 16
TILES = 64
EDGES = TILES * SLOTS
FEAT = 1024
ZERO_TILE = 3 * TILES
CHUNK = 32
ROWS = EDGES // 4
SHEET = 1024
GRAD_PITCH = ROWS + 8
UNROLL = 16
ENERGY_UNROLL = 4
NT = (((1,), (1,)), ((), ()))


def left_lanes(shape):
    return lax.broadcasted_iota(jnp.int32, shape, len(shape) - 1) < ORB


def swap(value):
    return pltpu.roll(value, ORB, value.ndim - 1)


def turn_lanes(strip):
    lane = lax.broadcasted_iota(jnp.int32, strip[0].shape, 1)
    low = lane < 64
    even = lane % 64 < 32
    half = [None] * 4
    for r in range(2):
        half[r] = jnp.where(low, strip[r], pltpu.roll(strip[r + 2], 64, 1))
        half[r + 2] = jnp.where(low, pltpu.roll(strip[r], 64, 1), strip[r + 2])
    turned = [None] * 4
    for r in (0, 2):
        turned[r] = jnp.where(even, half[r], pltpu.roll(half[r + 1], 32, 1))
        turned[r + 1] = jnp.where(even, pltpu.roll(half[r], 96, 1), half[r + 1])
    return turned


def grad_blocks_kernel(
    index, tiles, rows, total, prev, own, following, weighted, out, table, left, strips, sems, *, part, factor
):
    step = pl.program_id(0)

    @pl.when(step == 0)
    def _():
        mine = own.at[:, pl.ds(part * CHUNK, CHUNK), :]
        copies = [
            pltpu.make_async_copy(src, table.at[pl.ds(n * TILES, TILES)], sems.at[n])
            for n, src in enumerate((prev, mine, following))
        ]
        copies.append(pltpu.make_async_copy(weighted, left, sems.at[3]))
        for copy in copies:
            copy.start()
        table[ZERO_TILE] = jnp.zeros((CHUNK, BANDS), jnp.bfloat16)

        def clear(n, carry):
            strips[pl.ds(pl.multiple_of(n * 128, 8), 128), :] = jnp.zeros((128, 128), jnp.float32)
            return carry

        lax.fori_loop(0, ORB * GRAD_PITCH // 128, clear, 0)
        for copy in copies:
            copy.wait()

        def item_body(n, carry):
            at = [rows[n * UNROLL + u] for u in range(UNROLL)]
            who = [tiles[n * UNROLL + u] for u in range(UNROLL)]
            which = [[index[row * 4 + p] for p in range(4)] for row in at]
            products = [
                lax.dot_general(
                    left[who[u]],
                    jnp.concatenate([table[w] for w in which[u]], axis=0),
                    NT,
                    preferred_element_type=jnp.float32,
                )
                for u in range(UNROLL)
            ]
            for row, product in zip(at, products):
                strips[pl.ds(row, ORB, stride=GRAD_PITCH), :] = product
            return carry

        lax.fori_loop(0, (total[0] + UNROLL - 1) // UNROLL, item_body, 0)

    quads = out.shape[1] // 128
    group = 128

    def group_body(g, carry):
        for quad in range(quads):
            base = (step * quads + quad) * 4 * GRAD_PITCH + g * group
            strip = [
                strips[pl.ds(pl.multiple_of(base + r * GRAD_PITCH, 8), group), :] * factor
                for r in range(4)
            ]
            turned = [t.reshape(group // 8, 1, 8, 128) for t in turn_lanes(strip)]
            both = jnp.concatenate(turned, axis=1).reshape(group * 4, 128)
            spot = pl.ds(pl.multiple_of(g * (group * 4), 16), group * 4)
            out[spot, quad * 128 : (quad + 1) * 128] = both.astype(jnp.bfloat16)
        return carry

    lax.fori_loop(0, ROWS // group, group_body, 0)


def grad_blocks(plan, prev, own, following, weighted, part, factor):
    block = 512
    return pl.pallas_call(
        functools.partial(grad_blocks_kernel, part=part, factor=factor),
        grid_spec=pltpu.PrefetchScalarGridSpec(
            num_scalar_prefetch=4,
            grid=(ORB * CHUNK // block,),
            in_specs=[pl.BlockSpec(memory_space=pltpu.MemorySpace.HBM)] * 4,
            out_specs=pl.BlockSpec((EDGES, block), lambda j, *_: (0, j)),
            scratch_shapes=[
                pltpu.VMEM((ZERO_TILE + 1, CHUNK, BANDS), jnp.bfloat16),
                pltpu.VMEM((TILES, ORB, BANDS), jnp.bfloat16),
                pltpu.VMEM((ORB * GRAD_PITCH, 128), jnp.float32),
                pltpu.SemaphoreType.DMA((4,)),
            ],
        ),
        out_shape=jax.ShapeDtypeStruct((EDGES, ORB * CHUNK), jnp.bfloat16),
        compiler_params=pltpu.CompilerParams(vmem_limit_bytes=60 * 2**20),
        cost_estimate=pl.CostEstimate(
            flops=8 * EDGES * ORB * CHUNK * BANDS, bytes_accessed=12 * 2**20, transcendentals=0
        ),
        name="grad_blocks",
    )(*plan, prev, own, following, weighted)


def plan_items(index, counts):
    each = (counts + 3) // 4
    ends = jnp.cumsum(each)
    item = jnp.arange(ROWS, dtype=jnp.int32)
    tile = jnp.sum((ends[None, :] <= item[:, None]).astype(jnp.int32), axis=1)
    hit = lax.broadcasted_iota(jnp.int32, (ROWS, TILES), 1) == tile[:, None]
    start = jnp.sum(jnp.where(hit, (ends - each)[None, :], 0), axis=1)
    used = item < ends[-1]
    rows = jnp.where(used, tile * 4 + item - start, ROWS)
    slots = jnp.concatenate([index.reshape(-1), jnp.full((16,), ZERO_TILE, jnp.int32)])
    return slots, jnp.where(used, tile, 0), rows, ends[-1:]


def energy_kernel(
    index, tiles, rows, total, who, prev0, prev1, own, following0, following1, mine, theirs, *rest, factor
):
    sheets, (out, table, strips, near, far, weights, sems) = rest[:8], rest[8:]
    low = left_lanes((ROWS, 128))
    places = (
        (prev0, table.at[pl.ds(0, TILES), pl.ds(0, CHUNK)]),
        (prev1, table.at[pl.ds(0, TILES), pl.ds(CHUNK, CHUNK)]),
        (own, table.at[pl.ds(TILES, TILES)]),
        (following0, table.at[pl.ds(2 * TILES, TILES), pl.ds(0, CHUNK)]),
        (following1, table.at[pl.ds(2 * TILES, TILES), pl.ds(CHUNK, CHUNK)]),
    )
    late = [pltpu.make_async_copy(src, dst, sems.at[n]) for n, (src, dst) in enumerate(places)]
    early = [
        pltpu.make_async_copy(mine, near, sems.at[5]),
        pltpu.make_async_copy(theirs, far, sems.at[6]),
    ]
    for n, sheet in enumerate(sheets):
        spot = weights.at[n // 4, pl.ds(n % 4 * SHEET, SHEET)]
        early.append(pltpu.make_async_copy(sheet, spot, sems.at[7 + n]))
    for copy in early + late:
        copy.start()
    table[ZERO_TILE] = jnp.zeros((ORB, BANDS), jnp.bfloat16)
    for part in (0, 1):
        strips[pl.ds(part * GRAD_PITCH + ROWS, ORB, stride=2 * GRAD_PITCH), :] = jnp.zeros(
            (ORB, 128), jnp.float32
        )
    for copy in early:
        copy.wait()

    def pair_body(n, carry):
        spot = pl.ds(pl.multiple_of(n * 128, 128), 128)
        product = lax.dot_general(
            near[...], weights[0, spot, :], NT, preferred_element_type=jnp.float32
        ) + lax.dot_general(far[...], weights[1, spot, :], NT, preferred_element_type=jnp.float32)
        product = product.reshape(TILES // 2, 4, 8, 128)
        one, two = (pl.multiple_of(who[2 * n + u] * (2 * GRAD_PITCH), 8) for u in (0, 1))
        for part in (0, 1):
            front = product[:, 2 * part].reshape(ROWS, 128)
            back = product[:, 2 * part + 1].reshape(ROWS, 128)
            strips[pl.ds(one + part * GRAD_PITCH, ROWS), :] = jnp.where(low, front, swap(back))
            strips[pl.ds(two + part * GRAD_PITCH, ROWS), :] = jnp.where(low, swap(front), back)
        return carry

    lax.fori_loop(0, ORB // 2, pair_body, 0, unroll=2)
    for copy in late:
        copy.wait()

    def item_body(n, carry):
        at = [rows[n * ENERGY_UNROLL + u] for u in range(ENERGY_UNROLL)]
        home = [tiles[n * ENERGY_UNROLL + u] for u in range(ENERGY_UNROLL)]
        which = [[index[row * 4 + p] for p in range(4)] for row in at]
        for u in range(ENERGY_UNROLL):
            left = jnp.concatenate(
                [
                    strips[
                        pl.ds(part * GRAD_PITCH + at[u], ORB, stride=2 * GRAD_PITCH), :
                    ].astype(jnp.bfloat16)
                    for part in (0, 1)
                ],
                axis=1,
            )
            right = jnp.concatenate([table[w] for w in which[u]], axis=0)
            applied = jnp.dot(left, right, preferred_element_type=jnp.float32)
            terms = table[TILES + home[u]].astype(jnp.float32) * applied
            carry = carry + jnp.sum(terms.reshape(8, 8, BANDS), axis=0)
        return carry

    trips = (total[0] + ENERGY_UNROLL - 1) // ENERGY_UNROLL
    sums = lax.fori_loop(0, trips, item_body, jnp.zeros((8, BANDS), jnp.float32))
    out[...] = jnp.sum(sums, axis=0, keepdims=True) * factor


def energy_share(plan, who, prev, own, following, mine, theirs, sheets, factor):
    return pl.pallas_call(
        functools.partial(energy_kernel, factor=factor),
        grid_spec=pltpu.PrefetchScalarGridSpec(
            num_scalar_prefetch=5,
            grid=(1,),
            in_specs=[pl.BlockSpec(memory_space=pltpu.MemorySpace.HBM)] * 15,
            out_specs=pl.BlockSpec((1, BANDS), lambda j, *_: (0, 0)),
            scratch_shapes=[
                pltpu.VMEM((ZERO_TILE + 1, ORB, BANDS), jnp.bfloat16),
                pltpu.VMEM((2 * ORB * GRAD_PITCH, 128), jnp.float32),
                pltpu.VMEM((EDGES, FEAT // 2), jnp.bfloat16),
                pltpu.VMEM((EDGES, FEAT // 2), jnp.bfloat16),
                pltpu.VMEM((2, 4 * SHEET, FEAT // 2), jnp.bfloat16),
                pltpu.SemaphoreType.DMA((15,)),
            ],
        ),
        out_shape=jax.ShapeDtypeStruct((1, BANDS), jnp.float32),
        compiler_params=pltpu.CompilerParams(vmem_limit_bytes=60 * 2**20),
        cost_estimate=pl.CostEstimate(
            flops=2 * EDGES * ORB * ORB * (FEAT + BANDS * 4), bytes_accessed=16 * 2**20, transcendentals=0
        ),
        name="energy_share",
    )(*plan, who, *prev, own, *following, mine, theirs, *sheets)


def ring(axis, hop):
    pairs = []
    for i in range(64):
        spot = [i // 16, i // 4 % 4, i % 4]
        spot[axis] = (spot[axis] + hop) % 4
        pairs.append((i, spot[0] * 16 + spot[1] * 4 + spot[2]))
    return pairs


def spread(value, axis):
    return [value] + [lax.ppermute(value, "space", ring(axis, hop)) for hop in (1, 2, 3)]


def step(features, psi, neighbors, counts, occupation, weights):
    nspace = lax.axis_size("space")
    myself = lax.axis_index("space")
    core = lax.axis_index("dp")
    factor = 1.0 / math.sqrt(TILES * nspace * SLOTS)
    own = psi.reshape(TILES, ORB, BANDS)
    up = [(i, (i + 1) % nspace) for i in range(nspace)]
    down = [(j, i) for i, j in up]
    prev0 = lax.ppermute(own[:, :CHUNK], "space", up)
    following0 = lax.ppermute(own[:, :CHUNK], "space", down)
    half = FEAT // 2
    swapped = [(0, 1), (1, 0)]
    sheet = lax.dynamic_slice_in_dim(weights.T, core * half, half, 1)
    sheet = jnp.concatenate(spread(sheet, 2), axis=0)
    sheet = jnp.concatenate(spread(sheet, 1), axis=0)
    sheets = spread(sheet, 0)
    sheets = sheets + [lax.ppermute(sheet, "dp", swapped) for sheet in sheets]
    back = jnp.arange(ORB, dtype=jnp.int32)
    who = (
        (myself // 16 - back // 16) % 4 * 16
        + (myself // 4 - back // 4) % 4 * 4
        + (myself - back) % 4
    ).astype(jnp.int32)
    second, prev0, following0 = lax.optimization_barrier((own[:, CHUNK:], prev0, following0))
    prev1 = lax.ppermute(second, "space", up)
    following1 = lax.ppermute(second, "space", down)
    prev, following = (prev0, prev1), (following0, following1)

    where = neighbors.reshape(TILES, SLOTS)
    placed = (where // TILES - myself + 1 + nspace) % nspace * TILES + where % TILES
    slot = lax.broadcasted_iota(jnp.int32, (TILES, SLOTS), 1)
    used = counts.reshape(TILES)
    plan = plan_items(jnp.where(slot < used[:, None], placed, ZERO_TILE), used)
    weighted = (own.astype(jnp.float32) * occupation).astype(jnp.bfloat16)
    edges = (
        features.reshape(TILES // 2, 2, 4, 4, FEAT).transpose(0, 3, 1, 2, 4).reshape(EDGES, FEAT)
    )

    theirs = lax.dynamic_slice_in_dim(edges, (1 - core) * half, half, 1)
    mine = lax.dynamic_slice_in_dim(edges, core * half, half, 1)
    over_edges = (((0,), (0,)), ((), ()))
    arrived = []
    for part in (0, 1):
        blocks = grad_blocks(plan, prev[part], own, following[part], weighted, part, factor)
        send = lax.dot_general(blocks, theirs, over_edges, preferred_element_type=jnp.float32)
        other = lax.ppermute(send.astype(jnp.bfloat16), "dp", swapped)
        keep = lax.dot_general(blocks, mine, over_edges, preferred_element_type=jnp.float32)
        summed = (keep + other.astype(jnp.float32)).astype(jnp.bfloat16)
        parts = lax.all_to_all(summed, "space", 0, 0, tiled=True)
        arrived.append(parts)
    partial = energy_share(plan, who, prev, own, following, mine, theirs, sheets, factor)
    energies = partial
    for axis, place in ((2, myself % 4), (1, myself // 4 % 4), (0, myself // 16)):
        pieces = jnp.concatenate(spread(energies, axis), axis=0)
        energies = sum(
            lax.dynamic_slice_in_dim(pieces, (place - spot) % 4, 1, 0) for spot in range(4)
        )
    shares = [
        jnp.sum(parts.reshape(nspace, CHUNK, half).astype(jnp.float32), axis=0) for parts in arrived
    ]
    gradient = lax.all_gather(jnp.concatenate(shares, axis=0), "dp", axis=1, tiled=True)
    return (energies, gradient)


def solution(mesh):
    placed = (
        P("dp", "space", None, None),
        P("dp", "space", None, None),
        P("dp", "space", None),
        P("dp", "space"),
        P("dp", None),
        P(None, "space"),
    )
    return jax.shard_map(
        step,
        mesh=mesh,
        in_specs=placed,
        out_specs=(P("dp", None), P("space", None)),
        check_vma=False,
    )
```

```python
import functools
import math

import jax
import jax.numpy as jnp
from jax import lax
from jax.experimental import pallas as pl
from jax.experimental.pallas import tpu as pltpu
from jax.sharding import PartitionSpec as P


ORB = 64
BANDS = 256
SLOTS = 16
TILES = 64
EDGES = TILES * SLOTS
FEAT = 1024
ZERO_TILE = 3 * TILES
ROWS = EDGES // 4
SHEET = 1024
GRAD_PITCH = ROWS + 8
UNROLL = 8
ENERGY_UNROLL = 4
NT = (((1,), (1,)), ((), ()))


def left_lanes(shape):
    return lax.broadcasted_iota(jnp.int32, shape, len(shape) - 1) < ORB


def swap(value):
    return pltpu.roll(value, ORB, value.ndim - 1)


def grad_blocks_kernel(
    index, tiles, rows, total, prev, own, following, weighted, out, table, left, strips, sems, *, factor
):
    step = pl.program_id(0)

    @pl.when(step == 0)
    def _():
        copies = [
            pltpu.make_async_copy(src, table.at[pl.ds(n * TILES, TILES)], sems.at[n])
            for n, src in enumerate((prev, own, following))
        ]
        copies.append(pltpu.make_async_copy(weighted, left, sems.at[3]))
        for copy in copies:
            copy.start()
        table[ZERO_TILE] = jnp.zeros((ORB, BANDS), jnp.bfloat16)

        def clear(n, carry):
            strips[pl.ds(pl.multiple_of(n * 256, 8), 256), :] = jnp.zeros((256, 128), jnp.float32)
            return carry

        lax.fori_loop(0, 2 * ORB * GRAD_PITCH // 256, clear, 0)
        for copy in copies:
            copy.wait()

        def item_body(n, carry):
            at = [rows[n * UNROLL + u] for u in range(UNROLL)]
            home = [tiles[n * UNROLL + u] for u in range(UNROLL)]
            which = [[index[row * 4 + p] for p in range(4)] for row in at]
            products = [
                lax.dot_general(
                    left[home[u]],
                    jnp.concatenate([table[w] for w in which[u]], axis=0),
                    NT,
                    preferred_element_type=jnp.float32,
                )
                for u in range(UNROLL)
            ]
            for row, product in zip(at, products):
                for part in (0, 1):
                    strips[pl.ds(part * GRAD_PITCH + row, ORB, stride=2 * GRAD_PITCH), :] = product[
                        :, part * 128 : (part + 1) * 128
                    ]
            return carry

        lax.fori_loop(0, (total[0] + UNROLL - 1) // UNROLL, item_body, 0)

    pairs = out.shape[1] // 128
    group = 64
    low = left_lanes((group, 128))

    def group_body(g, carry):
        for pair in range(pairs):
            base = (step * pairs + pair) * 4 * GRAD_PITCH + g * group
            turned = []
            for part in (0, 1):
                spot = base + part * GRAD_PITCH
                one = strips[pl.ds(pl.multiple_of(spot, 8), group), :] * factor
                spot = spot + 2 * GRAD_PITCH
                two = strips[pl.ds(pl.multiple_of(spot, 8), group), :] * factor
                turned.append(jnp.where(low, one, swap(two)).reshape(group // 8, 1, 8, 128))
                turned.append(jnp.where(low, swap(one), two).reshape(group // 8, 1, 8, 128))
            both = jnp.concatenate(turned, axis=1).reshape(group * 4, 128)
            spot = pl.ds(pl.multiple_of(g * (group * 4), 16), group * 4)
            out[spot, pair * 128 : (pair + 1) * 128] = both.astype(jnp.bfloat16)
        return carry

    lax.fori_loop(0, ROWS // group, group_body, 0)


def grad_blocks(plan, prev, own, following, weighted, factor):
    block = 512
    return pl.pallas_call(
        functools.partial(grad_blocks_kernel, factor=factor),
        grid_spec=pltpu.PrefetchScalarGridSpec(
            num_scalar_prefetch=4,
            grid=(ORB * ORB // block,),
            in_specs=[pl.BlockSpec(memory_space=pltpu.MemorySpace.HBM)] * 4,
            out_specs=pl.BlockSpec((EDGES, block), lambda j, *_: (0, j)),
            scratch_shapes=[
                pltpu.VMEM((ZERO_TILE + 1, ORB, BANDS), jnp.bfloat16),
                pltpu.VMEM((TILES, ORB, BANDS), jnp.bfloat16),
                pltpu.VMEM((2 * ORB * GRAD_PITCH, 128), jnp.float32),
                pltpu.SemaphoreType.DMA((4,)),
            ],
        ),
        out_shape=jax.ShapeDtypeStruct((EDGES, ORB * ORB), jnp.bfloat16),
        compiler_params=pltpu.CompilerParams(vmem_limit_bytes=60 * 2**20),
        cost_estimate=pl.CostEstimate(
            flops=8 * EDGES * ORB * ORB * BANDS, bytes_accessed=16 * 2**20, transcendentals=0
        ),
        name="grad_blocks",
    )(*plan, prev, own, following, weighted)


def plan_items(index, counts):
    each = (counts + 3) // 4
    ends = jnp.cumsum(each)
    item = jnp.arange(ROWS, dtype=jnp.int32)
    tile = jnp.sum((ends[None, :] <= item[:, None]).astype(jnp.int32), axis=1)
    hit = lax.broadcasted_iota(jnp.int32, (ROWS, TILES), 1) == tile[:, None]
    start = jnp.sum(jnp.where(hit, (ends - each)[None, :], 0), axis=1)
    used = item < ends[-1]
    rows = jnp.where(used, tile * 4 + item - start, ROWS)
    slots = jnp.concatenate([index.reshape(-1), jnp.full((16,), ZERO_TILE, jnp.int32)])
    return slots, jnp.where(used, tile, 0), rows, ends[-1:]


def energy_kernel(
    index, tiles, rows, total, who, prev, own, following, mine, theirs, *rest, factor
):
    sheets, (out, table, strips, near, far, weights, sems) = rest[:8], rest[8:]
    low = left_lanes((ROWS, 128))
    late = [
        pltpu.make_async_copy(src, table.at[pl.ds(n * TILES, TILES)], sems.at[n])
        for n, src in enumerate((prev, own, following))
    ]
    early = [
        pltpu.make_async_copy(mine, near, sems.at[3]),
        pltpu.make_async_copy(theirs, far, sems.at[4]),
    ]
    for n, sheet in enumerate(sheets):
        spot = weights.at[n // 4, pl.ds(n % 4 * SHEET, SHEET)]
        early.append(pltpu.make_async_copy(sheet, spot, sems.at[5 + n]))
    for copy in early + late:
        copy.start()
    table[ZERO_TILE] = jnp.zeros((ORB, BANDS), jnp.bfloat16)
    for part in (0, 1):
        strips[pl.ds(part * GRAD_PITCH + ROWS, ORB, stride=2 * GRAD_PITCH), :] = jnp.zeros(
            (ORB, 128), jnp.float32
        )
    for copy in early:
        copy.wait()

    def pair_body(n, carry):
        spot = pl.ds(pl.multiple_of(n * 128, 128), 128)
        product = lax.dot_general(
            near[...], weights[0, spot, :], NT, preferred_element_type=jnp.float32
        ) + lax.dot_general(far[...], weights[1, spot, :], NT, preferred_element_type=jnp.float32)
        product = product.reshape(TILES // 2, 4, 8, 128)
        one, two = (pl.multiple_of(who[2 * n + u] * (2 * GRAD_PITCH), 8) for u in (0, 1))
        for part in (0, 1):
            front = product[:, 2 * part].reshape(ROWS, 128)
            back = product[:, 2 * part + 1].reshape(ROWS, 128)
            strips[pl.ds(one + part * GRAD_PITCH, ROWS), :] = jnp.where(low, front, swap(back))
            strips[pl.ds(two + part * GRAD_PITCH, ROWS), :] = jnp.where(low, swap(front), back)
        return carry

    lax.fori_loop(0, ORB // 2, pair_body, 0, unroll=2)
    for copy in late:
        copy.wait()

    def item_body(n, carry):
        at = [rows[n * ENERGY_UNROLL + u] for u in range(ENERGY_UNROLL)]
        home = [tiles[n * ENERGY_UNROLL + u] for u in range(ENERGY_UNROLL)]
        which = [[index[row * 4 + p] for p in range(4)] for row in at]
        for u in range(ENERGY_UNROLL):
            left = jnp.concatenate(
                [
                    strips[
                        pl.ds(part * GRAD_PITCH + at[u], ORB, stride=2 * GRAD_PITCH), :
                    ].astype(jnp.bfloat16)
                    for part in (0, 1)
                ],
                axis=1,
            )
            right = jnp.concatenate([table[w] for w in which[u]], axis=0)
            applied = jnp.dot(left, right, preferred_element_type=jnp.float32)
            terms = table[TILES + home[u]].astype(jnp.float32) * applied
            carry = carry + jnp.sum(terms.reshape(8, 8, BANDS), axis=0)
        return carry

    trips = (total[0] + ENERGY_UNROLL - 1) // ENERGY_UNROLL
    sums = lax.fori_loop(0, trips, item_body, jnp.zeros((8, BANDS), jnp.float32))
    out[...] = jnp.sum(sums, axis=0, keepdims=True) * factor


def energy_share(plan, who, prev, own, following, mine, theirs, sheets, factor):
    return pl.pallas_call(
        functools.partial(energy_kernel, factor=factor),
        grid_spec=pltpu.PrefetchScalarGridSpec(
            num_scalar_prefetch=5,
            grid=(1,),
            in_specs=[pl.BlockSpec(memory_space=pltpu.MemorySpace.HBM)] * 13,
            out_specs=pl.BlockSpec((1, BANDS), lambda j, *_: (0, 0)),
            scratch_shapes=[
                pltpu.VMEM((ZERO_TILE + 1, ORB, BANDS), jnp.bfloat16),
                pltpu.VMEM((2 * ORB * GRAD_PITCH, 128), jnp.float32),
                pltpu.VMEM((EDGES, FEAT // 2), jnp.bfloat16),
                pltpu.VMEM((EDGES, FEAT // 2), jnp.bfloat16),
                pltpu.VMEM((2, 4 * SHEET, FEAT // 2), jnp.bfloat16),
                pltpu.SemaphoreType.DMA((13,)),
            ],
        ),
        out_shape=jax.ShapeDtypeStruct((1, BANDS), jnp.float32),
        compiler_params=pltpu.CompilerParams(vmem_limit_bytes=60 * 2**20),
        cost_estimate=pl.CostEstimate(
            flops=2 * EDGES * ORB * ORB * (FEAT + BANDS * 4), bytes_accessed=16 * 2**20, transcendentals=0
        ),
        name="energy_share",
    )(*plan, who, prev, own, following, mine, theirs, *sheets)


def ring(axis, hop):
    pairs = []
    for i in range(64):
        spot = [i // 16, i // 4 % 4, i % 4]
        spot[axis] = (spot[axis] + hop) % 4
        pairs.append((i, spot[0] * 16 + spot[1] * 4 + spot[2]))
    return pairs


def spread(value, axis):
    return [value] + [lax.ppermute(value, "space", ring(axis, hop)) for hop in (1, 2, 3)]


def step(features, psi, neighbors, counts, occupation, weights):
    nspace = lax.axis_size("space")
    myself = lax.axis_index("space")
    core = lax.axis_index("dp")
    factor = 1.0 / math.sqrt(TILES * nspace * SLOTS)
    own = psi.reshape(TILES, ORB, BANDS)
    up = [(i, (i + 1) % nspace) for i in range(nspace)]
    down = [(j, i) for i, j in up]
    prev = lax.ppermute(own, "space", up)
    following = lax.ppermute(own, "space", down)
    half = FEAT // 2
    swapped = [(0, 1), (1, 0)]
    sheet = lax.dynamic_slice_in_dim(weights.T, core * half, half, 1)
    sheet = jnp.concatenate(spread(sheet, 2), axis=0)
    sheet = jnp.concatenate(spread(sheet, 1), axis=0)
    sheets = spread(sheet, 0)
    sheets = sheets + [lax.ppermute(sheet, "dp", swapped) for sheet in sheets]
    back = jnp.arange(ORB, dtype=jnp.int32)
    who = (
        (myself // 16 - back // 16) % 4 * 16
        + (myself // 4 - back // 4) % 4 * 4
        + (myself - back) % 4
    ).astype(jnp.int32)
    where = neighbors.reshape(TILES, SLOTS)
    placed = (where // TILES - myself + 1 + nspace) % nspace * TILES + where % TILES
    slot = lax.broadcasted_iota(jnp.int32, (TILES, SLOTS), 1)
    used = counts.reshape(TILES)
    plan = plan_items(jnp.where(slot < used[:, None], placed, ZERO_TILE), used)
    weighted = (own.astype(jnp.float32) * occupation).astype(jnp.bfloat16)
    edges = (
        features.reshape(TILES // 2, 2, 4, 4, FEAT).transpose(0, 3, 1, 2, 4).reshape(EDGES, FEAT)
    )

    theirs = lax.dynamic_slice_in_dim(edges, (1 - core) * half, half, 1)
    mine = lax.dynamic_slice_in_dim(edges, core * half, half, 1)
    over_edges = (((0,), (0,)), ((), ()))
    blocks = grad_blocks(plan, prev, own, following, weighted, factor)
    send = lax.dot_general(blocks, theirs, over_edges, preferred_element_type=jnp.float32)
    other = lax.ppermute(send.astype(jnp.bfloat16), "dp", swapped)
    keep = lax.dot_general(blocks, mine, over_edges, preferred_element_type=jnp.float32)
    summed = (keep + other.astype(jnp.float32)).astype(jnp.bfloat16)
    parts = lax.all_to_all(summed, "space", 0, 0, tiled=True)
    partial = energy_share(plan, who, prev, own, following, mine, theirs, sheets, factor)
    energies = partial
    for axis, place in ((2, myself % 4), (1, myself // 4 % 4), (0, myself // 16)):
        pieces = jnp.concatenate(spread(energies, axis), axis=0)
        energies = sum(
            lax.dynamic_slice_in_dim(pieces, (place - spot) % 4, 1, 0) for spot in range(4)
        )
    share = jnp.sum(parts.reshape(nspace, ORB, half).astype(jnp.float32), axis=0)
    gradient = lax.all_gather(share, "dp", axis=1, tiled=True)
    return (energies, gradient)


def solution(mesh):
    placed = (
        P("dp", "space", None, None),
        P("dp", "space", None, None),
        P("dp", "space", None),
        P("dp", "space"),
        P("dp", None),
        P(None, "space"),
    )
    return jax.shard_map(
        step,
        mesh=mesh,
        in_specs=placed,
        out_specs=(P("dp", None), P("space", None)),
        check_vma=False,
    )
```

```python
import functools
import math

import jax
import jax.numpy as jnp
from jax import lax
from jax.experimental import pallas as pl
from jax.experimental.pallas import tpu as pltpu
from jax.sharding import PartitionSpec as P

ORB = 64
BANDS = 256
SLOTS = 16
TILES = 64
EDGES = TILES * SLOTS
FEAT = 1024
ZERO_TILE = 3 * TILES
ROWS = EDGES // 4
GRAD_PITCH = ROWS + 8
UNROLL = 8
ENERGY_UNROLL = 8
NT = (((1,), (1,)), ((), ()))


def left_lanes(shape):
    return lax.broadcasted_iota(jnp.int32, shape, len(shape) - 1) < ORB


def swap(value):
    return pltpu.roll(value, ORB, value.ndim - 1)


def grad_blocks_kernel(
    index, tiles, rows, total, prev, own, following, weighted, out, table, left, strips, sems, *, factor
):
    step = pl.program_id(0)

    @pl.when(step == 0)
    def _():
        copies = [
            pltpu.make_async_copy(src, table.at[pl.ds(n * TILES, TILES)], sems.at[n])
            for n, src in enumerate((prev, own, following))
        ]
        copies.append(pltpu.make_async_copy(weighted, left, sems.at[3]))
        for copy in copies:
            copy.start()
        table[ZERO_TILE] = jnp.zeros((ORB, BANDS), jnp.bfloat16)

        def clear(n, carry):
            strips[pl.ds(pl.multiple_of(n * 256, 8), 256), :] = jnp.zeros((256, 128), jnp.float32)
            return carry

        lax.fori_loop(0, 2 * ORB * GRAD_PITCH // 256, clear, 0)
        for copy in copies:
            copy.wait()

        def item_body(n, carry):
            at = [rows[n * UNROLL + u] for u in range(UNROLL)]
            home = [tiles[n * UNROLL + u] for u in range(UNROLL)]
            which = [[index[row * 4 + p] for p in range(4)] for row in at]
            products = [
                lax.dot_general(
                    left[home[u]],
                    jnp.concatenate([table[w] for w in which[u]], axis=0),
                    NT,
                    preferred_element_type=jnp.float32,
                )
                for u in range(UNROLL)
            ]
            for row, product in zip(at, products):
                for part in (0, 1):
                    strips[pl.ds(part * GRAD_PITCH + row, ORB, stride=2 * GRAD_PITCH), :] = product[
                        :, part * 128 : (part + 1) * 128
                    ]
            return carry

        lax.fori_loop(0, (total[0] + UNROLL - 1) // UNROLL, item_body, 0)

    pairs = out.shape[1] // 128
    group = 64
    low = left_lanes((group, 128))

    def group_body(g, carry):
        for pair in range(pairs):
            base = (step * pairs + pair) * 4 * GRAD_PITCH + g * group
            turned = []
            for part in (0, 1):
                spot = base + part * GRAD_PITCH
                one = strips[pl.ds(pl.multiple_of(spot, 8), group), :] * factor
                spot = spot + 2 * GRAD_PITCH
                two = strips[pl.ds(pl.multiple_of(spot, 8), group), :] * factor
                turned.append(jnp.where(low, one, swap(two)).reshape(group // 8, 1, 8, 128))
                turned.append(jnp.where(low, swap(one), two).reshape(group // 8, 1, 8, 128))
            both = jnp.concatenate(turned, axis=1).reshape(group * 4, 128)
            spot = pl.ds(pl.multiple_of(g * (group * 4), 16), group * 4)
            out[spot, pair * 128 : (pair + 1) * 128] = both.astype(jnp.bfloat16)
        return carry

    lax.fori_loop(0, ROWS // group, group_body, 0)


def grad_blocks(plan, prev, own, following, weighted, factor):
    block = 512
    return pl.pallas_call(
        functools.partial(grad_blocks_kernel, factor=factor),
        grid_spec=pltpu.PrefetchScalarGridSpec(
            num_scalar_prefetch=4,
            grid=(ORB * ORB // block,),
            in_specs=[pl.BlockSpec(memory_space=pltpu.MemorySpace.HBM)] * 4,
            out_specs=pl.BlockSpec((EDGES, block), lambda j, *_: (0, j)),
            scratch_shapes=[
                pltpu.VMEM((ZERO_TILE + 1, ORB, BANDS), jnp.bfloat16),
                pltpu.VMEM((TILES, ORB, BANDS), jnp.bfloat16),
                pltpu.VMEM((2 * ORB * GRAD_PITCH, 128), jnp.float32),
                pltpu.SemaphoreType.DMA((4,)),
            ],
        ),
        out_shape=jax.ShapeDtypeStruct((EDGES, ORB * ORB), jnp.bfloat16),
        compiler_params=pltpu.CompilerParams(vmem_limit_bytes=60 * 2**20),
        cost_estimate=pl.CostEstimate(
            flops=8 * EDGES * ORB * ORB * BANDS, bytes_accessed=16 * 2**20, transcendentals=0
        ),
        name="grad_blocks",
    )(*plan, prev, own, following, weighted)


def plan_items(index, counts):
    each = (counts + 3) // 4
    ends = jnp.cumsum(each)
    item = jnp.arange(ROWS, dtype=jnp.int32)
    tile = jnp.sum((ends[None, :] <= item[:, None]).astype(jnp.int32), axis=1)
    hit = lax.broadcasted_iota(jnp.int32, (ROWS, TILES), 1) == tile[:, None]
    start = jnp.sum(jnp.where(hit, (ends - each)[None, :], 0), axis=1)
    used = item < ends[-1]
    rows = jnp.where(used, tile * 4 + item - start, ROWS)
    slots = jnp.concatenate([index.reshape(-1), jnp.full((16,), ZERO_TILE, jnp.int32)])
    return slots, jnp.where(used, tile, 0), rows, ends[-1:]


def energy_kernel(
    index, tiles, rows, total, prev, own, following, mine, theirs, *rest, factor
):
    sheets, (out, table, strips, near, far, weights, sems) = rest[:2], rest[2:]
    low = left_lanes((ROWS, 128))
    late = [
        pltpu.make_async_copy(src, table.at[pl.ds(n * TILES, TILES)], sems.at[n])
        for n, src in enumerate((prev, own, following))
    ]
    early = [
        pltpu.make_async_copy(mine, near, sems.at[3]),
        pltpu.make_async_copy(theirs, far, sems.at[4]),
    ]
    for n, sheet in enumerate(sheets):
        early.append(pltpu.make_async_copy(sheet, weights.at[n], sems.at[5 + n]))
    for copy in early + late:
        copy.start()
    table[ZERO_TILE] = jnp.zeros((ORB, BANDS), jnp.bfloat16)
    for part in (0, 1):
        strips[pl.ds(part * GRAD_PITCH + ROWS, ORB, stride=2 * GRAD_PITCH), :] = jnp.zeros(
            (ORB, 128), jnp.float32
        )
    for copy in early:
        copy.wait()

    def quad_body(n, carry):
        spot = pl.ds(pl.multiple_of(n * 256, 256), 256)
        product = lax.dot_general(
            near[...], weights[0, spot, :], NT, preferred_element_type=jnp.float32
        ) + lax.dot_general(far[...], weights[1, spot, :], NT, preferred_element_type=jnp.float32)
        for pair in (0, 1):
            piece = product[:, pair * 128 : (pair + 1) * 128].reshape(TILES // 2, 4, 8, 128)
            base = (4 * n + 2 * pair) * (2 * GRAD_PITCH)
            for part in (0, 1):
                front = piece[:, 2 * part].reshape(ROWS, 128)
                back = piece[:, 2 * part + 1].reshape(ROWS, 128)
                one = pl.multiple_of(base + part * GRAD_PITCH, 8)
                two = pl.multiple_of(base + (2 + part) * GRAD_PITCH, 8)
                strips[pl.ds(one, ROWS), :] = jnp.where(low, front, swap(back))
                strips[pl.ds(two, ROWS), :] = jnp.where(low, swap(front), back)
        return carry

    lax.fori_loop(0, ORB // 4, quad_body, 0)
    for copy in late:
        copy.wait()

    def item_body(n, carry):
        at = [rows[n * ENERGY_UNROLL + u] for u in range(ENERGY_UNROLL)]
        home = [tiles[n * ENERGY_UNROLL + u] for u in range(ENERGY_UNROLL)]
        which = [[index[row * 4 + p] for p in range(4)] for row in at]
        for u in range(ENERGY_UNROLL):
            left = jnp.concatenate(
                [
                    strips[
                        pl.ds(part * GRAD_PITCH + at[u], ORB, stride=2 * GRAD_PITCH), :
                    ].astype(jnp.bfloat16)
                    for part in (0, 1)
                ],
                axis=1,
            )
            right = jnp.concatenate([table[w] for w in which[u]], axis=0)
            applied = jnp.dot(left, right, preferred_element_type=jnp.float32)
            terms = table[TILES + home[u]].astype(jnp.float32) * applied
            carry = carry + jnp.sum(terms.reshape(8, 8, BANDS), axis=0)
        return carry

    trips = (total[0] + ENERGY_UNROLL - 1) // ENERGY_UNROLL
    sums = lax.fori_loop(0, trips, item_body, jnp.zeros((8, BANDS), jnp.float32))
    out[...] = jnp.sum(sums, axis=0, keepdims=True) * factor


def energy_share(plan, prev, own, following, mine, theirs, sheets, factor):
    return pl.pallas_call(
        functools.partial(energy_kernel, factor=factor),
        grid_spec=pltpu.PrefetchScalarGridSpec(
            num_scalar_prefetch=4,
            grid=(1,),
            in_specs=[pl.BlockSpec(memory_space=pltpu.MemorySpace.HBM)] * 7,
            out_specs=pl.BlockSpec((1, BANDS), lambda j, *_: (0, 0)),
            scratch_shapes=[
                pltpu.VMEM((ZERO_TILE + 1, ORB, BANDS), jnp.bfloat16),
                pltpu.VMEM((2 * ORB * GRAD_PITCH, 128), jnp.float32),
                pltpu.VMEM((EDGES, FEAT // 2), jnp.bfloat16),
                pltpu.VMEM((EDGES, FEAT // 2), jnp.bfloat16),
                pltpu.VMEM((2, ORB * ORB, FEAT // 2), jnp.bfloat16),
                pltpu.SemaphoreType.DMA((7,)),
            ],
        ),
        out_shape=jax.ShapeDtypeStruct((1, BANDS), jnp.float32),
        compiler_params=pltpu.CompilerParams(vmem_limit_bytes=60 * 2**20),
        cost_estimate=pl.CostEstimate(
            flops=2 * EDGES * ORB * ORB * (FEAT + BANDS * 4), bytes_accessed=16 * 2**20, transcendentals=0
        ),
        name="energy_share",
    )(*plan, prev, own, following, mine, theirs, *sheets)


def ring(axis, hop):
    pairs = []
    for i in range(64):
        spot = [i // 16, i // 4 % 4, i % 4]
        spot[axis] = (spot[axis] + hop) % 4
        pairs.append((i, spot[0] * 16 + spot[1] * 4 + spot[2]))
    return pairs


def spread(value, axis):
    return [value] + [lax.ppermute(value, "space", ring(axis, hop)) for hop in (1, 2, 3)]


def step(features, psi, neighbors, counts, occupation, weights):
    nspace = lax.axis_size("space")
    myself = lax.axis_index("space")
    core = lax.axis_index("dp")
    factor = 1.0 / math.sqrt(TILES * nspace * SLOTS)
    own = psi.reshape(TILES, ORB, BANDS)
    up = [(i, (i + 1) % nspace) for i in range(nspace)]
    down = [(j, i) for i, j in up]
    prev = lax.ppermute(own, "space", up)
    following = lax.ppermute(own, "space", down)
    half = FEAT // 2
    swapped = [(0, 1), (1, 0)]
    sheet = lax.dynamic_slice_in_dim(weights.T, core * half, half, 1)
    sheet = lax.all_gather(sheet, "space", axis=0, tiled=True)
    sheets = (sheet, lax.ppermute(sheet, "dp", swapped))

    where = neighbors.reshape(TILES, SLOTS)
    placed = (where // TILES - myself + 1 + nspace) % nspace * TILES + where % TILES
    slot = lax.broadcasted_iota(jnp.int32, (TILES, SLOTS), 1)
    used = counts.reshape(TILES)
    plan = plan_items(jnp.where(slot < used[:, None], placed, ZERO_TILE), used)
    weighted = (own.astype(jnp.float32) * occupation).astype(jnp.bfloat16)
    edges = (
        features.reshape(TILES // 2, 2, 4, 4, FEAT).transpose(0, 3, 1, 2, 4).reshape(EDGES, FEAT)
    )

    theirs = lax.dynamic_slice_in_dim(edges, (1 - core) * half, half, 1)
    mine = lax.dynamic_slice_in_dim(edges, core * half, half, 1)
    over_edges = (((0,), (0,)), ((), ()))
    blocks = grad_blocks(plan, prev, own, following, weighted, factor)
    send = lax.dot_general(blocks, theirs, over_edges, preferred_element_type=jnp.float32)
    other = lax.ppermute(send.astype(jnp.bfloat16), "dp", swapped)
    keep = lax.dot_general(blocks, mine, over_edges, preferred_element_type=jnp.float32)
    summed = (keep + other.astype(jnp.float32)).astype(jnp.bfloat16)
    parts = lax.all_to_all(summed, "space", 0, 0, tiled=True)
    partial = energy_share(plan, prev, own, following, mine, theirs, sheets, factor)
    energies = partial
    for axis, place in ((2, myself % 4), (1, myself // 4 % 4), (0, myself // 16)):
        pieces = jnp.concatenate(spread(energies, axis), axis=0)
        energies = sum(
            lax.dynamic_slice_in_dim(pieces, (place - spot) % 4, 1, 0) for spot in range(4)
        )
    share = jnp.sum(parts.reshape(nspace, ORB, half).astype(jnp.float32), axis=0)
    gradient = lax.all_gather(share, "dp", axis=1, tiled=True)
    return (energies, gradient)


def solution(mesh):
    placed = (
        P("dp", "space", None, None),
        P("dp", "space", None, None),
        P("dp", "space", None),
        P("dp", "space"),
        P("dp", None),
        P(None, "space"),
    )
    return jax.shard_map(
        step,
        mesh=mesh,
        in_specs=placed,
        out_specs=(P("dp", None), P("space", None)),
        check_vma=False,
    )
```

```python
import functools
import math

import jax
import jax.numpy as jnp
from jax import lax
from jax.experimental import pallas as pl
from jax.experimental.pallas import tpu as pltpu
from jax.sharding import PartitionSpec as P


ORB = 64
BANDS = 256
SLOTS = 16
TILES = 64
EDGES = TILES * SLOTS
FEAT = 1024
ZERO_TILE = 3 * TILES
ROWS = EDGES // 4
SHEET = 1024
GRAD_PITCH = ROWS + 8
UNROLL = 8
ENERGY_UNROLL = 8
NT = (((1,), (1,)), ((), ()))


def left_lanes(shape):
    return lax.broadcasted_iota(jnp.int32, shape, len(shape) - 1) < ORB


def swap(value):
    return pltpu.roll(value, ORB, value.ndim - 1)


def grad_blocks_kernel(
    index, tiles, rows, total, prev, own, following, weighted, out, table, left, strips, sems, *, factor
):
    step = pl.program_id(0)

    @pl.when(step == 0)
    def _():
        copies = [
            pltpu.make_async_copy(src, table.at[pl.ds(n * TILES, TILES)], sems.at[n])
            for n, src in enumerate((prev, own, following))
        ]
        copies.append(pltpu.make_async_copy(weighted, left, sems.at[3]))
        for copy in copies:
            copy.start()
        table[ZERO_TILE] = jnp.zeros((ORB, BANDS), jnp.bfloat16)

        def clear(n, carry):
            strips[pl.ds(pl.multiple_of(n * 256, 8), 256), :] = jnp.zeros((256, 128), jnp.float32)
            return carry

        lax.fori_loop(0, 2 * ORB * GRAD_PITCH // 256, clear, 0)
        for copy in copies:
            copy.wait()

        def item_body(n, carry):
            at = [rows[n * UNROLL + u] for u in range(UNROLL)]
            home = [tiles[n * UNROLL + u] for u in range(UNROLL)]
            which = [[index[row * 4 + p] for p in range(4)] for row in at]
            products = [
                lax.dot_general(
                    left[home[u]],
                    jnp.concatenate([table[w] for w in which[u]], axis=0),
                    NT,
                    preferred_element_type=jnp.float32,
                )
                for u in range(UNROLL)
            ]
            for row, product in zip(at, products):
                for part in (0, 1):
                    strips[pl.ds(part * GRAD_PITCH + row, ORB, stride=2 * GRAD_PITCH), :] = product[
                        :, part * 128 : (part + 1) * 128
                    ]
            return carry

        lax.fori_loop(0, (total[0] + UNROLL - 1) // UNROLL, item_body, 0)

    pairs = out.shape[1] // 128
    group = 64
    low = left_lanes((group, 128))

    def group_body(g, carry):
        for pair in range(pairs):
            base = (step * pairs + pair) * 4 * GRAD_PITCH + g * group
            turned = []
            for part in (0, 1):
                spot = base + part * GRAD_PITCH
                one = strips[pl.ds(pl.multiple_of(spot, 8), group), :] * factor
                spot = spot + 2 * GRAD_PITCH
                two = strips[pl.ds(pl.multiple_of(spot, 8), group), :] * factor
                turned.append(jnp.where(low, one, swap(two)).reshape(group // 8, 1, 8, 128))
                turned.append(jnp.where(low, swap(one), two).reshape(group // 8, 1, 8, 128))
            both = jnp.concatenate(turned, axis=1).reshape(group * 4, 128)
            spot = pl.ds(pl.multiple_of(g * (group * 4), 16), group * 4)
            out[spot, pair * 128 : (pair + 1) * 128] = both.astype(jnp.bfloat16)
        return carry

    lax.fori_loop(0, ROWS // group, group_body, 0)


def grad_blocks(plan, prev, own, following, weighted, factor):
    block = 512
    return pl.pallas_call(
        functools.partial(grad_blocks_kernel, factor=factor),
        grid_spec=pltpu.PrefetchScalarGridSpec(
            num_scalar_prefetch=4,
            grid=(ORB * ORB // block,),
            in_specs=[pl.BlockSpec(memory_space=pltpu.MemorySpace.HBM)] * 4,
            out_specs=pl.BlockSpec((EDGES, block), lambda j, *_: (0, j)),
            scratch_shapes=[
                pltpu.VMEM((ZERO_TILE + 1, ORB, BANDS), jnp.bfloat16),
                pltpu.VMEM((TILES, ORB, BANDS), jnp.bfloat16),
                pltpu.VMEM((2 * ORB * GRAD_PITCH, 128), jnp.float32),
                pltpu.SemaphoreType.DMA((4,)),
            ],
        ),
        out_shape=jax.ShapeDtypeStruct((EDGES, ORB * ORB), jnp.bfloat16),
        compiler_params=pltpu.CompilerParams(vmem_limit_bytes=60 * 2**20),
        cost_estimate=pl.CostEstimate(
            flops=8 * EDGES * ORB * ORB * BANDS, bytes_accessed=16 * 2**20, transcendentals=0
        ),
        name="grad_blocks",
    )(*plan, prev, own, following, weighted)


def plan_items(index, counts):
    each = (counts + 3) // 4
    ends = jnp.cumsum(each)
    item = jnp.arange(ROWS, dtype=jnp.int32)
    tile = jnp.sum((ends[None, :] <= item[:, None]).astype(jnp.int32), axis=1)
    hit = lax.broadcasted_iota(jnp.int32, (ROWS, TILES), 1) == tile[:, None]
    start = jnp.sum(jnp.where(hit, (ends - each)[None, :], 0), axis=1)
    used = item < ends[-1]
    rows = jnp.where(used, tile * 4 + item - start, ROWS)
    slots = jnp.concatenate([index.reshape(-1), jnp.full((16,), ZERO_TILE, jnp.int32)])
    return slots, jnp.where(used, tile, 0), rows, ends[-1:]


def energy_kernel(
    index, tiles, rows, total, who, prev, own, following, mine, theirs, *rest, factor
):
    sheets, (out, table, strips, near, far, weights, sems) = rest[:8], rest[8:]
    low = left_lanes((ROWS, 128))
    late = [
        pltpu.make_async_copy(src, table.at[pl.ds(n * TILES, TILES)], sems.at[n])
        for n, src in enumerate((prev, own, following))
    ]
    early = [
        pltpu.make_async_copy(mine, near, sems.at[3]),
        pltpu.make_async_copy(theirs, far, sems.at[4]),
    ]
    for n, sheet in enumerate(sheets):
        spot = weights.at[n // 4, pl.ds(n % 4 * SHEET, SHEET)]
        early.append(pltpu.make_async_copy(sheet, spot, sems.at[5 + n]))
    for copy in early + late:
        copy.start()
    table[ZERO_TILE] = jnp.zeros((ORB, BANDS), jnp.bfloat16)
    for part in (0, 1):
        strips[pl.ds(part * GRAD_PITCH + ROWS, ORB, stride=2 * GRAD_PITCH), :] = jnp.zeros(
            (ORB, 128), jnp.float32
        )
    for copy in early:
        copy.wait()

    def quad_body(n, carry):
        spot = pl.ds(pl.multiple_of(n * 256, 256), 256)
        product = lax.dot_general(
            near[...], weights[0, spot, :], NT, preferred_element_type=jnp.float32
        ) + lax.dot_general(far[...], weights[1, spot, :], NT, preferred_element_type=jnp.float32)
        for pair in (0, 1):
            piece = product[:, pair * 128 : (pair + 1) * 128].reshape(TILES // 2, 4, 8, 128)
            bases = [who[4 * n + 2 * pair + u] * (2 * GRAD_PITCH) for u in (0, 1)]
            for part in (0, 1):
                front = piece[:, 2 * part].reshape(ROWS, 128)
                back = piece[:, 2 * part + 1].reshape(ROWS, 128)
                one = pl.multiple_of(bases[0] + part * GRAD_PITCH, 8)
                two = pl.multiple_of(bases[1] + part * GRAD_PITCH, 8)
                strips[pl.ds(one, ROWS), :] = jnp.where(low, front, swap(back))
                strips[pl.ds(two, ROWS), :] = jnp.where(low, swap(front), back)
        return carry

    lax.fori_loop(0, ORB // 4, quad_body, 0)
    for copy in late:
        copy.wait()

    def item_body(n, carry):
        at = [rows[n * ENERGY_UNROLL + u] for u in range(ENERGY_UNROLL)]
        home = [tiles[n * ENERGY_UNROLL + u] for u in range(ENERGY_UNROLL)]
        which = [[index[row * 4 + p] for p in range(4)] for row in at]
        for u in range(ENERGY_UNROLL):
            left = jnp.concatenate(
                [
                    strips[
                        pl.ds(part * GRAD_PITCH + at[u], ORB, stride=2 * GRAD_PITCH), :
                    ].astype(jnp.bfloat16)
                    for part in (0, 1)
                ],
                axis=1,
            )
            right = jnp.concatenate([table[w] for w in which[u]], axis=0)
            applied = jnp.dot(left, right, preferred_element_type=jnp.float32)
            terms = table[TILES + home[u]].astype(jnp.float32) * applied
            carry = carry + jnp.sum(terms.reshape(8, 8, BANDS), axis=0)
        return carry

    trips = (total[0] + ENERGY_UNROLL - 1) // ENERGY_UNROLL
    sums = lax.fori_loop(0, trips, item_body, jnp.zeros((8, BANDS), jnp.float32))
    out[...] = jnp.sum(sums, axis=0, keepdims=True) * factor


def energy_share(plan, who, prev, own, following, mine, theirs, sheets, factor):
    return pl.pallas_call(
        functools.partial(energy_kernel, factor=factor),
        grid_spec=pltpu.PrefetchScalarGridSpec(
            num_scalar_prefetch=5,
            grid=(1,),
            in_specs=[pl.BlockSpec(memory_space=pltpu.MemorySpace.HBM)] * 13,
            out_specs=pl.BlockSpec((1, BANDS), lambda j, *_: (0, 0)),
            scratch_shapes=[
                pltpu.VMEM((ZERO_TILE + 1, ORB, BANDS), jnp.bfloat16),
                pltpu.VMEM((2 * ORB * GRAD_PITCH, 128), jnp.float32),
                pltpu.VMEM((EDGES, FEAT // 2), jnp.bfloat16),
                pltpu.VMEM((EDGES, FEAT // 2), jnp.bfloat16),
                pltpu.VMEM((2, ORB * ORB, FEAT // 2), jnp.bfloat16),
                pltpu.SemaphoreType.DMA((13,)),
            ],
        ),
        out_shape=jax.ShapeDtypeStruct((1, BANDS), jnp.float32),
        compiler_params=pltpu.CompilerParams(vmem_limit_bytes=60 * 2**20),
        cost_estimate=pl.CostEstimate(
            flops=2 * EDGES * ORB * ORB * (FEAT + BANDS * 4), bytes_accessed=16 * 2**20, transcendentals=0
        ),
        name="energy_share",
    )(*plan, who, prev, own, following, mine, theirs, *sheets)


def ring(axis, hop):
    pairs = []
    for i in range(64):
        spot = [i // 16, i // 4 % 4, i % 4]
        spot[axis] = (spot[axis] + hop) % 4
        pairs.append((i, spot[0] * 16 + spot[1] * 4 + spot[2]))
    return pairs


def spread(value, axis):
    return [value] + [lax.ppermute(value, "space", ring(axis, hop)) for hop in (1, 2, 3)]


def step(features, psi, neighbors, counts, occupation, weights):
    nspace = lax.axis_size("space")
    myself = lax.axis_index("space")
    core = lax.axis_index("dp")
    factor = 1.0 / math.sqrt(TILES * nspace * SLOTS)
    own = psi.reshape(TILES, ORB, BANDS)
    up = [(i, (i + 1) % nspace) for i in range(nspace)]
    down = [(j, i) for i, j in up]
    prev = lax.ppermute(own, "space", up)
    following = lax.ppermute(own, "space", down)
    half = FEAT // 2
    swapped = [(0, 1), (1, 0)]
    sheet = lax.dynamic_slice_in_dim(weights.T, core * half, half, 1)
    sheet = jnp.concatenate(spread(sheet, 2), axis=0)
    sheet = jnp.concatenate(spread(sheet, 1), axis=0)
    sheets = spread(sheet, 0)
    sheets = sheets + [lax.ppermute(sheet, "dp", swapped) for sheet in sheets]
    back = jnp.arange(ORB, dtype=jnp.int32)
    who = (
        (myself // 16 - back // 16) % 4 * 16
        + (myself // 4 - back // 4) % 4 * 4
        + (myself - back) % 4
    ).astype(jnp.int32)

    where = neighbors.reshape(TILES, SLOTS)
    placed = (where // TILES - myself + 1 + nspace) % nspace * TILES + where % TILES
    slot = lax.broadcasted_iota(jnp.int32, (TILES, SLOTS), 1)
    used = counts.reshape(TILES)
    plan = plan_items(jnp.where(slot < used[:, None], placed, ZERO_TILE), used)
    weighted = (own.astype(jnp.float32) * occupation).astype(jnp.bfloat16)
    edges = (
        features.reshape(TILES // 2, 2, 4, 4, FEAT).transpose(0, 3, 1, 2, 4).reshape(EDGES, FEAT)
    )

    theirs = lax.dynamic_slice_in_dim(edges, (1 - core) * half, half, 1)
    mine = lax.dynamic_slice_in_dim(edges, core * half, half, 1)
    over_edges = (((0,), (0,)), ((), ()))
    blocks = grad_blocks(plan, prev, own, following, weighted, factor)
    pieces = [blocks[:, : blocks.shape[1] // 2], blocks[:, blocks.shape[1] // 2 :]]
    others = []
    for piece in pieces:
        send = lax.dot_general(piece, theirs, over_edges, preferred_element_type=jnp.float32)
        others.append(lax.ppermute(send.astype(jnp.bfloat16), "dp", swapped))
    summed = []
    for piece, other in zip(pieces, others):
        keep = lax.dot_general(piece, mine, over_edges, preferred_element_type=jnp.float32)
        summed.append((keep + other.astype(jnp.float32)).astype(jnp.bfloat16))
    summed = jnp.concatenate(summed, axis=0)
    parts = lax.all_to_all(summed, "space", 0, 0, tiled=True)
    partial = energy_share(plan, who, prev, own, following, mine, theirs, sheets, factor)
    energies = partial
    for axis, place in ((2, myself % 4), (1, myself // 4 % 4), (0, myself // 16)):
        pieces = jnp.concatenate(spread(energies, axis), axis=0)
        energies = sum(
            lax.dynamic_slice_in_dim(pieces, (place - spot) % 4, 1, 0) for spot in range(4)
        )
    share = jnp.sum(parts.reshape(nspace, ORB, half).astype(jnp.float32), axis=0)
    gradient = lax.all_gather(share, "dp", axis=1, tiled=True)
    return (energies, gradient)


def solution(mesh):
    placed = (
        P("dp", "space", None, None),
        P("dp", "space", None, None),
        P("dp", "space", None),
        P("dp", "space"),
        P("dp", None),
        P(None, "space"),
    )
    return jax.shard_map(
        step,
        mesh=mesh,
        in_specs=placed,
        out_specs=(P("dp", None), P("space", None)),
        check_vma=False,
    )
```

```python
import functools
import math

import jax
import jax.numpy as jnp
from jax import lax
from jax.experimental import pallas as pl
from jax.experimental.pallas import tpu as pltpu
from jax.sharding import PartitionSpec as P


ORB = 64
BANDS = 256
SLOTS = 16
TILES = 64
EDGES = TILES * SLOTS
FEAT = 1024
ZERO_TILE = 3 * TILES
ROWS = EDGES // 4
SHEET = 1024
GRAD_PITCH = ROWS + 8
UNROLL = 8
ENERGY_UNROLL = 8
NT = (((1,), (1,)), ((), ()))


def left_lanes(shape):
    return lax.broadcasted_iota(jnp.int32, shape, len(shape) - 1) < ORB


def swap(value):
    return pltpu.roll(value, ORB, value.ndim - 1)


def grad_blocks_kernel(
    index, tiles, rows, total, prev, own, following, weighted, out, table, left, strips, sems, *, factor
):
    step = pl.program_id(0)

    @pl.when(step == 0)
    def _():
        copies = [
            pltpu.make_async_copy(src, table.at[pl.ds(n * TILES, TILES)], sems.at[n])
            for n, src in enumerate((prev, own, following))
        ]
        copies.append(pltpu.make_async_copy(weighted, left, sems.at[3]))
        for copy in copies:
            copy.start()
        table[ZERO_TILE] = jnp.zeros((ORB, BANDS), jnp.bfloat16)

        def clear(n, carry):
            strips[pl.ds(pl.multiple_of(n * 256, 8), 256), :] = jnp.zeros((256, 128), jnp.float32)
            return carry

        lax.fori_loop(0, 2 * ORB * GRAD_PITCH // 256, clear, 0)
        for copy in copies:
            copy.wait()

        def item_body(n, carry):
            at = [rows[n * UNROLL + u] for u in range(UNROLL)]
            home = [tiles[n * UNROLL + u] for u in range(UNROLL)]
            which = [[index[row * 4 + p] for p in range(4)] for row in at]
            products = [
                lax.dot_general(
                    left[home[u]],
                    jnp.concatenate([table[w] for w in which[u]], axis=0),
                    NT,
                    preferred_element_type=jnp.float32,
                )
                for u in range(UNROLL)
            ]
            for row, product in zip(at, products):
                for part in (0, 1):
                    strips[pl.ds(part * GRAD_PITCH + row, ORB, stride=2 * GRAD_PITCH), :] = product[
                        :, part * 128 : (part + 1) * 128
                    ]
            return carry

        lax.fori_loop(0, (total[0] + UNROLL - 1) // UNROLL, item_body, 0)

    pairs = out.shape[1] // 128
    group = 64
    low = left_lanes((group, 128))

    def group_body(g, carry):
        for pair in range(pairs):
            base = (step * pairs + pair) * 4 * GRAD_PITCH + g * group
            turned = []
            for part in (0, 1):
                spot = base + part * GRAD_PITCH
                one = strips[pl.ds(pl.multiple_of(spot, 8), group), :] * factor
                spot = spot + 2 * GRAD_PITCH
                two = strips[pl.ds(pl.multiple_of(spot, 8), group), :] * factor
                turned.append(jnp.where(low, one, swap(two)).reshape(group // 8, 1, 8, 128))
                turned.append(jnp.where(low, swap(one), two).reshape(group // 8, 1, 8, 128))
            both = jnp.concatenate(turned, axis=1).reshape(group * 4, 128)
            spot = pl.ds(pl.multiple_of(g * (group * 4), 16), group * 4)
            out[spot, pair * 128 : (pair + 1) * 128] = both.astype(jnp.bfloat16)
        return carry

    lax.fori_loop(0, ROWS // group, group_body, 0)


def grad_blocks(plan, prev, own, following, weighted, factor):
    block = 512
    return pl.pallas_call(
        functools.partial(grad_blocks_kernel, factor=factor),
        grid_spec=pltpu.PrefetchScalarGridSpec(
            num_scalar_prefetch=4,
            grid=(ORB * ORB // block,),
            in_specs=[pl.BlockSpec(memory_space=pltpu.MemorySpace.HBM)] * 4,
            out_specs=pl.BlockSpec((EDGES, block), lambda j, *_: (0, j)),
            scratch_shapes=[
                pltpu.VMEM((ZERO_TILE + 1, ORB, BANDS), jnp.bfloat16),
                pltpu.VMEM((TILES, ORB, BANDS), jnp.bfloat16),
                pltpu.VMEM((2 * ORB * GRAD_PITCH, 128), jnp.float32),
                pltpu.SemaphoreType.DMA((4,)),
            ],
        ),
        out_shape=jax.ShapeDtypeStruct((EDGES, ORB * ORB), jnp.bfloat16),
        compiler_params=pltpu.CompilerParams(vmem_limit_bytes=60 * 2**20),
        cost_estimate=pl.CostEstimate(
            flops=8 * EDGES * ORB * ORB * BANDS, bytes_accessed=16 * 2**20, transcendentals=0
        ),
        name="grad_blocks",
    )(*plan, prev, own, following, weighted)


def plan_items(index, counts):
    each = (counts + 3) // 4
    ends = jnp.cumsum(each)
    item = jnp.arange(ROWS, dtype=jnp.int32)
    tile = jnp.sum((ends[None, :] <= item[:, None]).astype(jnp.int32), axis=1)
    hit = lax.broadcasted_iota(jnp.int32, (ROWS, TILES), 1) == tile[:, None]
    start = jnp.sum(jnp.where(hit, (ends - each)[None, :], 0), axis=1)
    used = item < ends[-1]
    rows = jnp.where(used, tile * 4 + item - start, ROWS)
    slots = jnp.concatenate([index.reshape(-1), jnp.full((16,), ZERO_TILE, jnp.int32)])
    return slots, jnp.where(used, tile, 0), rows, ends[-1:]


def energy_kernel(
    index, tiles, rows, total, who, prev, own, following, mine, theirs, *rest, factor
):
    sheets, (out, table, strips, near, far, weights, sems) = rest[:8], rest[8:]
    low = left_lanes((ROWS, 128))
    late = [
        pltpu.make_async_copy(src, table.at[pl.ds(n * TILES, TILES)], sems.at[n])
        for n, src in enumerate((prev, own, following))
    ]
    early = [
        pltpu.make_async_copy(mine, near, sems.at[3]),
        pltpu.make_async_copy(theirs, far, sems.at[4]),
    ]
    for n, sheet in enumerate(sheets):
        spot = weights.at[n // 4, pl.ds(n % 4 * SHEET, SHEET)]
        early.append(pltpu.make_async_copy(sheet, spot, sems.at[5 + n]))
    for copy in early + late:
        copy.start()
    table[ZERO_TILE] = jnp.zeros((ORB, BANDS), jnp.bfloat16)
    for part in (0, 1):
        strips[pl.ds(part * GRAD_PITCH + ROWS, ORB, stride=2 * GRAD_PITCH), :] = jnp.zeros(
            (ORB, 128), jnp.float32
        )
    for copy in early:
        copy.wait()

    def quad_body(n, carry):
        spot = pl.ds(pl.multiple_of(n * 256, 256), 256)
        product = lax.dot_general(
            near[...], weights[0, spot, :], NT, preferred_element_type=jnp.float32
        ) + lax.dot_general(far[...], weights[1, spot, :], NT, preferred_element_type=jnp.float32)
        for pair in (0, 1):
            piece = product[:, pair * 128 : (pair + 1) * 128].reshape(TILES // 2, 4, 8, 128)
            bases = [who[4 * n + 2 * pair + u] * (2 * GRAD_PITCH) for u in (0, 1)]
            for part in (0, 1):
                front = piece[:, 2 * part].reshape(ROWS, 128)
                back = piece[:, 2 * part + 1].reshape(ROWS, 128)
                one = pl.multiple_of(bases[0] + part * GRAD_PITCH, 8)
                two = pl.multiple_of(bases[1] + part * GRAD_PITCH, 8)
                strips[pl.ds(one, ROWS), :] = jnp.where(low, front, swap(back))
                strips[pl.ds(two, ROWS), :] = jnp.where(low, swap(front), back)
        return carry

    lax.fori_loop(0, ORB // 4, quad_body, 0)
    for copy in late:
        copy.wait()

    def item_body(n, carry):
        at = [rows[n * ENERGY_UNROLL + u] for u in range(ENERGY_UNROLL)]
        home = [tiles[n * ENERGY_UNROLL + u] for u in range(ENERGY_UNROLL)]
        which = [[index[row * 4 + p] for p in range(4)] for row in at]
        for u in range(ENERGY_UNROLL):
            left = jnp.concatenate(
                [
                    strips[
                        pl.ds(part * GRAD_PITCH + at[u], ORB, stride=2 * GRAD_PITCH), :
                    ].astype(jnp.bfloat16)
                    for part in (0, 1)
                ],
                axis=1,
            )
            right = jnp.concatenate([table[w] for w in which[u]], axis=0)
            applied = jnp.dot(left, right, preferred_element_type=jnp.float32)
            terms = table[TILES + home[u]].astype(jnp.float32) * applied
            carry = carry + jnp.sum(terms.reshape(8, 8, BANDS), axis=0)
        return carry

    trips = (total[0] + ENERGY_UNROLL - 1) // ENERGY_UNROLL
    sums = lax.fori_loop(0, trips, item_body, jnp.zeros((8, BANDS), jnp.float32))
    out[...] = jnp.sum(sums, axis=0, keepdims=True) * factor


def energy_share(plan, who, prev, own, following, mine, theirs, sheets, factor):
    return pl.pallas_call(
        functools.partial(energy_kernel, factor=factor),
        grid_spec=pltpu.PrefetchScalarGridSpec(
            num_scalar_prefetch=5,
            grid=(1,),
            in_specs=[pl.BlockSpec(memory_space=pltpu.MemorySpace.HBM)] * 13,
            out_specs=pl.BlockSpec((1, BANDS), lambda j, *_: (0, 0)),
            scratch_shapes=[
                pltpu.VMEM((ZERO_TILE + 1, ORB, BANDS), jnp.bfloat16),
                pltpu.VMEM((2 * ORB * GRAD_PITCH, 128), jnp.float32),
                pltpu.VMEM((EDGES, FEAT // 2), jnp.bfloat16),
                pltpu.VMEM((EDGES, FEAT // 2), jnp.bfloat16),
                pltpu.VMEM((2, ORB * ORB, FEAT // 2), jnp.bfloat16),
                pltpu.SemaphoreType.DMA((13,)),
            ],
        ),
        out_shape=jax.ShapeDtypeStruct((1, BANDS), jnp.float32),
        compiler_params=pltpu.CompilerParams(vmem_limit_bytes=60 * 2**20),
        cost_estimate=pl.CostEstimate(
            flops=2 * EDGES * ORB * ORB * (FEAT + BANDS * 4), bytes_accessed=16 * 2**20, transcendentals=0
        ),
        name="energy_share",
    )(*plan, who, prev, own, following, mine, theirs, *sheets)


def ring(axis, hop):
    pairs = []
    for i in range(64):
        spot = [i // 16, i // 4 % 4, i % 4]
        spot[axis] = (spot[axis] + hop) % 4
        pairs.append((i, spot[0] * 16 + spot[1] * 4 + spot[2]))
    return pairs


def spread(value, axis):
    return [value] + [lax.ppermute(value, "space", ring(axis, hop)) for hop in (1, 2, 3)]


def step(features, psi, neighbors, counts, occupation, weights):
    nspace = lax.axis_size("space")
    myself = lax.axis_index("space")
    core = lax.axis_index("dp")
    factor = 1.0 / math.sqrt(TILES * nspace * SLOTS)
    own = psi.reshape(TILES, ORB, BANDS)
    up = [(i, (i + 1) % nspace) for i in range(nspace)]
    down = [(j, i) for i, j in up]
    prev = lax.ppermute(own, "space", up)
    following = lax.ppermute(own, "space", down)
    half = FEAT // 2
    swapped = [(0, 1), (1, 0)]
    sheet = lax.dynamic_slice_in_dim(weights.T, core * half, half, 1)
    sheet = jnp.concatenate(spread(sheet, 2), axis=0)
    sheet = jnp.concatenate(spread(sheet, 1), axis=0)
    sheets = spread(sheet, 0)
    sheets = sheets + [lax.ppermute(sheet, "dp", swapped) for sheet in sheets]
    back = jnp.arange(ORB, dtype=jnp.int32)
    who = (
        (myself // 16 - back // 16) % 4 * 16
        + (myself // 4 - back // 4) % 4 * 4
        + (myself - back) % 4
    ).astype(jnp.int32)

    where = neighbors.reshape(TILES, SLOTS)
    placed = (where // TILES - myself + 1 + nspace) % nspace * TILES + where % TILES
    slot = lax.broadcasted_iota(jnp.int32, (TILES, SLOTS), 1)
    used = counts.reshape(TILES)
    plan = plan_items(jnp.where(slot < used[:, None], placed, ZERO_TILE), used)
    weighted = (own.astype(jnp.float32) * occupation).astype(jnp.bfloat16)
    edges = features.reshape(TILES // 2, 2, 4, 4, FEAT).transpose(0, 3, 1, 2, 4)
    edges = edges.reshape(EDGES, FEAT)

    theirs = lax.dynamic_slice_in_dim(edges, (1 - core) * half, half, 1)
    mine = lax.dynamic_slice_in_dim(edges, core * half, half, 1)
    over_edges = (((0,), (0,)), ((), ()))
    blocks = grad_blocks(plan, prev, own, following, weighted, factor)
    pieces = [blocks[:, : blocks.shape[1] // 2], blocks[:, blocks.shape[1] // 2 :]]
    others = []
    for piece in pieces:
        send = lax.dot_general(piece, theirs, over_edges, preferred_element_type=jnp.float32)
        others.append(lax.ppermute(send.astype(jnp.bfloat16), "dp", swapped))
    summed = []
    for piece, other in zip(pieces, others):
        keep = lax.dot_general(piece, mine, over_edges, preferred_element_type=jnp.float32)
        summed.append((keep + other.astype(jnp.float32)).astype(jnp.bfloat16))
    summed = jnp.concatenate(summed, axis=0)
    parts = lax.all_to_all(summed, "space", 0, 0, tiled=True)
    partial = energy_share(plan, who, prev, own, following, mine, theirs, sheets, factor)
    energies = partial
    for axis, place in ((2, myself % 4), (1, myself // 4 % 4), (0, myself // 16)):
        pieces = jnp.concatenate(spread(energies, axis), axis=0)
        energies = sum(
            lax.dynamic_slice_in_dim(pieces, (place - spot) % 4, 1, 0) for spot in range(4)
        )
    share = jnp.sum(parts.reshape(nspace, ORB, half).astype(jnp.float32), axis=0)
    gradient = lax.all_gather(share, "dp", axis=1, tiled=True)
    return (energies, gradient)


def solution(mesh):
    placed = (
        P("dp", "space", None, None),
        P("dp", "space", None, None),
        P("dp", "space", None),
        P("dp", "space"),
        P("dp", None),
        P(None, "space"),
    )
    return jax.shard_map(
        step,
        mesh=mesh,
        in_specs=placed,
        out_specs=(P("dp", None), P("space", None)),
        check_vma=False,
    )
```
